1024 devices in a mesh: layer: 64 (over z_lo, y), blk: 16 (over z_hi, x, core).
Axes of the slice: x: 4, y: 4, z: 32 (z_hi: 2, z_lo: 16; z = z_hi * 16 + z_lo), core: 2. Of those that a mesh axis runs over, the one named last changes fastest.
Arguments:
- train_in: float32 [64, 32, 64, 512], P('layer', 'blk'), may hold values from -6 to 6
- train_out: float32 [64, 32, 64, 512], P('layer', 'blk'), may hold values from -6 to 6
- query_in: bfloat16 [64, 16, 256, 512], P('layer', 'blk'), may hold values from -6 to 6
- query_out: bfloat16 [64, 16, 256, 512], P('layer', 'blk'), may hold values from -6 to 6
- basis_in: bfloat16 [64, 512, 512], P('layer'), may hold values from -0.25 to 0.25
- basis_out: bfloat16 [64, 512, 512], P('layer'), may hold values from -0.25 to 0.25
- eigen_values: float32 [64, 512, 512], P('layer'), may hold values from 0.05 to 5
- train_ids: int32 [32], P('blk'), may hold values from 0 to 31, each once
- query_ids: int32 [16], P('blk'), may hold values from 0 to 31
Outputs:
- scores: float32 [16, 32], P('blk')
The draws below stay inside these ranges and needn't reach their ends.
Inputs may be any that keep to these rules, and one draw needn't show every extreme that they name: `train_ids`: every training sequence index appears exactly once.
All inputs are finite; a program needn't handle non-finite values.
Results may differ from the reference program's by a relative error of at most 0.006.
Values may be sent and summed in bfloat16 or wider, within the bound.
No kernel may reach another device: no remote copies, remote signals or barrier semaphores. Data moves between devices by JAX's collectives and lax.ppermute only.
A program may use at most 32 MiB of HBM per device.

```python
import math
import jax
import jax.numpy as jnp
from jax import lax

KIN = 512
KOUT = 512
LEN = 64
QLEN = 256
BLOCKS = 64
TRAIN_SEQS = 32
QUERIES = 16


def place_ends(result, stream_key, least, high):
    place = [jax.random.randint(jax.random.fold_in(stream_key, axis), (), 0, length) for axis, length in enumerate(result.shape)]
    longest = result.shape.index(max(result.shape))
    beside = place[:longest] + [(place[longest] + 1) % result.shape[longest]] + place[longest + 1:]
    return result.at[tuple(place)].set(least).at[tuple(beside)].set(high)


def level_of(own_key, dims, cuts, smallest, largest):
    level = 1.0
    for axis_at, blocks in cuts:
        heights = jax.random.uniform(jax.random.fold_in(jax.random.fold_in(own_key, 6), axis_at), (blocks,), jnp.float32, smallest / len(cuts), largest / len(cuts))
        level = level * jnp.repeat(jnp.exp(heights), dims[axis_at] // blocks).reshape((-1,) + (1,) * (len(dims) - 1 - axis_at))
    return level


def gaussian(key, dims, width, bound, pieces=(), kind=jnp.bfloat16):
    result = width * jax.random.normal(key, dims, jnp.float32)
    if pieces:
        result = result * level_of(key, dims, pieces, -0.22, 0.18)
    return jnp.clip(result, -bound, bound).astype(kind)


def setup_inputs(seed: int = 0) -> dict:
    arg_keys = jax.random.split(jax.random.key(seed), 10)
    return {
        "train_in": gaussian(arg_keys[0], (BLOCKS, TRAIN_SEQS, LEN, KIN), 1.0, 6.0, ((0, 64), (1, 16)), jnp.float32),
        "train_out": gaussian(arg_keys[1], (BLOCKS, TRAIN_SEQS, LEN, KOUT), 1.0, 6.0, ((0, 64), (1, 16)), jnp.float32),
        "query_in": gaussian(arg_keys[2], (BLOCKS, QUERIES, QLEN, KIN), 1.0, 6.0, ((0, 64), (1, 16))),
        "query_out": gaussian(arg_keys[3], (BLOCKS, QUERIES, QLEN, KOUT), 1.0, 6.0, ((0, 64), (1, 16))),
        "basis_in": gaussian(arg_keys[4], (BLOCKS, KIN, KIN), KIN ** -0.5, 0.25, ((0, 64),)),
        "basis_out": gaussian(arg_keys[5], (BLOCKS, KOUT, KOUT), KOUT ** -0.5, 0.25, ((0, 64),)),
        "eigen_values": jnp.clip(jnp.exp(math.log(5.0) - 4.6051702 * jax.random.uniform(arg_keys[6], (BLOCKS, KOUT, KIN), jnp.float32) ** level_of(arg_keys[6], (BLOCKS, KOUT, KIN), ((0, 64),), -0.2, 0.2)), 0.05, 5.0),
        "train_ids": jax.random.permutation(arg_keys[7], TRAIN_SEQS).astype(jnp.int32),
        "query_ids": place_ends(jax.random.randint(arg_keys[8], (QUERIES,), 0, TRAIN_SEQS), jax.random.fold_in(arg_keys[8], 1), 0, TRAIN_SEQS - 1).astype(jnp.int32),
    }


damping = 0.1

def project(token_rows, eigen_basis):
    product = jnp.einsum('stk,ki->sti', token_rows.astype(jnp.float32), eigen_basis.astype(jnp.float32), precision=lax.Precision.HIGHEST)
    return product.astype(jnp.bfloat16)

def one_block(inputs):
    raw_in, raw_out, query_rows_in, query_rows_out, base_in, base_out, eigen_scales = inputs
    train_side_in = project(raw_in.astype(jnp.bfloat16), base_in)
    train_side_out = project(raw_out.astype(jnp.bfloat16), base_out)
    query_side_in = project(query_rows_in, base_in)
    query_side_out = project(query_rows_out, base_out)
    moment = jnp.einsum('qto,qti->qoi', query_side_out.astype(jnp.float32), query_side_in.astype(jnp.float32), precision=lax.Precision.HIGHEST)
    precond = (moment / (QLEN * (eigen_scales + damping))).astype(jnp.bfloat16)
    gradients = jnp.einsum('sto,sti->soi', train_side_out.astype(jnp.float32), train_side_in.astype(jnp.float32), precision=lax.Precision.HIGHEST)
    return jnp.einsum('qoi,soi->qs', precond.astype(jnp.float32), gradients, precision=lax.Precision.HIGHEST)

def reference(train_in, train_out, query_in, query_out, basis_in, basis_out, eigen_values, train_ids, query_ids):
    per_block = lax.map(one_block, (train_in, train_out, query_in, query_out, basis_in, basis_out, eigen_values))
    total = lax.optimization_barrier(jnp.sum(per_block, axis=0)) / math.sqrt(BLOCKS * KIN * KOUT)
    columns = jnp.arange(TRAIN_SEQS, dtype=jnp.int32)
    one_hot = (train_ids.astype(jnp.int32)[:, None] == columns[None, :]).astype(jnp.float32)
    scores = jnp.dot(total, one_hot, precision=lax.Precision.HIGHEST)
    return jnp.where(query_ids.astype(jnp.int32)[:, None] == columns[None, :], 0.0, scores)
```

```python
import math

import jax
import jax.numpy as jnp
from jax import lax
from jax.experimental import pallas as pl
from jax.experimental.pallas import tpu as pltpu
from jax.sharding import Mesh
from jax.sharding import PartitionSpec as P

damping = 0.1

ZLO, Y, ZHI, X, CORE = 16, 4, 2, 4, 2
NAMES = ("zlo", "y", "zhi", "x", "core")


def project(rows, basis):
    return jnp.dot(rows, basis, preferred_element_type=jnp.float32).astype(jnp.bfloat16)


def side_sums(tokens_ref, precond_refs, seqs, length):
    inside = tokens_ref[0].astype(jnp.float32)
    outside = tokens_ref[1]
    rows = []
    for ref in precond_refs:
        weighted = jnp.dot(outside, ref[...], preferred_element_type=jnp.float32)
        prod = weighted * inside
        rows.append(
            jnp.concatenate(
                [
                    jnp.sum(
                        jnp.sum(prod[s * length : (s + 1) * length], axis=0, keepdims=True),
                        axis=1,
                        keepdims=True,
                    )
                    for s in range(seqs)
                ],
                axis=1,
            )
        )
    return jnp.concatenate(rows, axis=0)


def place(sums, hot):
    total = sums[:, 0:1] * hot[0:1, :]
    for s in range(1, hot.shape[0]):
        total = total + sums[:, s : s + 1] * hot[s : s + 1, :]
    return total


def score_kernel(tokens_ref, hot_ref, *refs, length):
    out_ref = refs[-1]
    hot = hot_ref[...]
    out_ref[...] = place(side_sums(tokens_ref, refs[:-1], hot.shape[0], length), hot)


def scores_of(tokens, hot, preconds, length):
    vmem = pl.BlockSpec(memory_space=pltpu.VMEM)
    return pl.pallas_call(
        lambda *refs: score_kernel(*refs, length=length),
        out_shape=jax.ShapeDtypeStruct((len(preconds), hot.shape[1]), jnp.float32),
        in_specs=[vmem] * (2 + len(preconds)),
        out_specs=vmem,
        compiler_params=pltpu.CompilerParams(vmem_limit_bytes=40 << 20),
    )(tokens, hot, *preconds)


def gather_preconds(
    query_in, query_out, in_basis, out_basis, eigen_values, mine, hot, train_ids, length
):
    their_ids = lax.ppermute(train_ids, "zhi", [(0, 1), (1, 0)])
    side_in = project(query_in, in_basis)
    side_out = project(query_out, out_basis)
    moment = lax.dot_general(
        side_out, side_in, (((0,), (0,)), ((), ())), preferred_element_type=jnp.float32
    )
    scale = query_in.shape[0] * (eigen_values + damping)
    precond = (moment / scale).astype(jnp.bfloat16)
    along = [precond]
    for step in range(1, X):
        along.append(lax.ppermute(precond, "x", [(i, i ^ step) for i in range(X)]))
    beside = [lax.ppermute(p, "core", [(0, 1), (1, 0)]) for p in along]
    preconds = along + beside
    return preconds, scores_of(mine, hot, preconds, length), their_ids


def local(
    train_in,
    train_out,
    query_in,
    query_out,
    basis_in,
    basis_out,
    eigen_values,
    train_ids,
    query_ids,
):
    in_basis = basis_in[0]
    out_basis = basis_out[0]
    seqs, length, width = train_in.shape[1:]
    across = [(0, 1), (1, 0)]

    mine = jnp.stack(
        [
            project(train_in[0].astype(jnp.bfloat16).reshape(seqs * length, width), in_basis),
            project(train_out[0].astype(jnp.bfloat16).reshape(seqs * length, width), out_basis),
        ]
    )
    theirs = lax.ppermute(mine, "zhi", across)
    columns = jnp.arange(seqs * ZHI * X * CORE, dtype=jnp.int32)
    hot_mine = (train_ids[:, None] == columns[None, :]).astype(jnp.float32)
    preconds, partial_mine, their_ids = lax.cond(
        lax.axis_index("x") < X,
        lambda *ops: gather_preconds(*ops, length),
        lambda *ops: (
            [jnp.zeros((width, width), jnp.bfloat16)] * (X * CORE),
            jnp.zeros((X * CORE, columns.shape[0]), jnp.float32),
            train_ids,
        ),
        query_in[0, 0], query_out[0, 0], in_basis, out_basis, eigen_values[0], mine, hot_mine,
        train_ids,
    )
    hot_theirs = (their_ids[:, None] == columns[None, :]).astype(jnp.float32)
    partial_theirs = scores_of(theirs, hot_theirs, preconds, length)
    partial_value = partial_mine + partial_theirs

    k = jnp.arange(X * CORE, dtype=jnp.int32)
    owner = (lax.axis_index("x") ^ (k % X)) * CORE + (lax.axis_index("core") ^ (k // X))
    order = owner[None, :] == k[:, None]
    ordered = jnp.sum(
        jnp.where(order[:, :, None], partial_value[None, :, :], 0.0), axis=1
    )
    spread = jnp.broadcast_to(ordered[None], (Y,) + ordered.shape).reshape(Y * X * CORE, -1)
    near = jnp.sum(lax.all_to_all(spread, ("y", "x", "core"), 0, 0), axis=0)
    far = jnp.broadcast_to(near[None], (ZLO,) + near.shape)
    summed = jnp.sum(lax.all_to_all(far, "zlo", 0, 0), axis=0)
    factor = 1.0 / math.sqrt(ZLO * Y * in_basis.shape[0] * out_basis.shape[0])
    scores = (summed * factor)[None, :]
    return jnp.where(query_ids[:, None] == columns[None, :], 0.0, scores)


def solution(mesh):
    split = Mesh(mesh.devices.reshape(ZLO, Y, ZHI, X, CORE), NAMES)
    layer, blk = ("zlo", "y"), ("zhi", "x", "core")
    placed = (
        P(layer, blk, None, None),
        P(layer, blk, None, None),
        P(layer, blk, None, None),
        P(layer, blk, None, None),
        P(layer, None, None),
        P(layer, None, None),
        P(layer, None, None),
        P(blk),
        P(blk),
    )
    return jax.shard_map(
        local, mesh=split, in_specs=placed, out_specs=P(blk, None), check_vma=False
    )
```

```python
import math

import jax
import jax.numpy as jnp
from jax import lax
from jax.experimental import pallas as pl
from jax.experimental.pallas import tpu as pltpu
from jax.sharding import Mesh
from jax.sharding import PartitionSpec as P

damping = 0.1

ZLO, Y, ZHI, X, CORE = 16, 4, 2, 4, 2
NAMES = ("zlo", "y", "zhi", "x", "core")
SWAP = [(0, 1), (1, 0)]
EXTRA = 8

VMEM = pl.BlockSpec(memory_space=pltpu.VMEM)
SMEM = pl.BlockSpec(memory_space=pltpu.SMEM)


def project(rows, basis):
    return jnp.dot(rows, basis, preferred_element_type=jnp.float32).astype(jnp.bfloat16)


def train_kernel(ids_ref, in_ref, out_ref, in_basis_ref, out_basis_ref, packed_ref):
    tokens = in_ref.shape[0]
    packed_ref[:tokens] = project(in_ref[...].astype(jnp.bfloat16), in_basis_ref[...])
    packed_ref[tokens : 2 * tokens] = project(out_ref[...].astype(jnp.bfloat16), out_basis_ref[...])
    row = lax.broadcasted_iota(jnp.int32, (EXTRA, in_ref.shape[1]), 0)
    lane = lax.broadcasted_iota(jnp.int32, (EXTRA, in_ref.shape[1]), 1)
    hit = (row == 0) & (lane == ids_ref[0])
    for s in range(1, ids_ref.shape[0]):
        hit = hit | ((row == s) & (lane == ids_ref[s]))
    packed_ref[2 * tokens :] = jnp.where(hit, 1.0, 0.0).astype(jnp.bfloat16)


def pack_train(train_ids, train_in, train_out, in_basis, out_basis):
    tokens, width = train_in.shape
    return pl.pallas_call(
        train_kernel,
        out_shape=jax.ShapeDtypeStruct((2 * tokens + EXTRA, width), jnp.bfloat16),
        in_specs=[SMEM] + [VMEM] * 4,
        out_specs=VMEM,
    )(train_ids, train_in, train_out, in_basis, out_basis)


def score_kernel(packed_ref, *refs, length, columns):
    out_ref = refs[-1]
    tokens = (packed_ref.shape[0] - EXTRA) // 2
    seqs = tokens // length
    inside = packed_ref[:tokens].astype(jnp.float32)
    outside = packed_ref[tokens : 2 * tokens]
    hot = packed_ref[2 * tokens :].astype(jnp.float32)
    rows = [[] for _ in range(seqs)]
    for ref in refs[:-1]:
        weighted = jnp.dot(outside, ref[...], preferred_element_type=jnp.float32)
        prod = weighted * inside
        for s in range(seqs):
            rows[s].append(jnp.sum(prod[s * length : (s + 1) * length], axis=0, keepdims=True))
    total = None
    for s in range(seqs):
        sums = jnp.sum(jnp.concatenate(rows[s], axis=0), axis=1, keepdims=True)
        placed = sums * hot[s : s + 1, :columns]
        total = placed if total is None else total + placed
    out_ref[...] = total


def scores_of(packed, preconds, length, columns):
    return pl.pallas_call(
        lambda *refs: score_kernel(*refs, length=length, columns=columns),
        out_shape=jax.ShapeDtypeStruct((len(preconds), columns), jnp.float32),
        in_specs=[VMEM] * (1 + len(preconds)),
        out_specs=VMEM,
        compiler_params=pltpu.CompilerParams(vmem_limit_bytes=40 << 20),
    )(packed, *preconds)


def gather_preconds(query_in, query_out, in_basis, out_basis, eigen_values, mine, length, columns):
    side_in = project(query_in, in_basis)
    side_out = project(query_out, out_basis)
    moment = lax.dot_general(
        side_out, side_in, (((0,), (0,)), ((), ())), preferred_element_type=jnp.float32
    )
    scale = query_in.shape[0] * (eigen_values + damping)
    precond = (moment / scale).astype(jnp.bfloat16)
    along = [precond]
    for step in range(1, X):
        along.append(lax.ppermute(precond, "x", [(i, i ^ step) for i in range(X)]))
    beside = [lax.ppermute(p, "core", SWAP) for p in along]
    preconds = along + beside
    return preconds, scores_of(mine, preconds, length, columns)


def local(
    train_in,
    train_out,
    query_in,
    query_out,
    basis_in,
    basis_out,
    eigen_values,
    train_ids,
    query_ids,
):
    in_basis = basis_in[0]
    out_basis = basis_out[0]
    seqs, length, width = train_in.shape[1:]
    columns = seqs * ZHI * X * CORE
    tokens = (seqs * length, width)

    mine = pack_train(
        train_ids, train_in[0].reshape(tokens), train_out[0].reshape(tokens), in_basis, out_basis
    )
    theirs = lax.ppermute(mine, "zhi", SWAP)
    preconds, partial_mine = lax.cond(
        lax.axis_index("x") < X,
        lambda *ops: gather_preconds(*ops, length, columns),
        lambda *ops: (
            [jnp.zeros((width, width), jnp.bfloat16)] * (X * CORE),
            jnp.zeros((X * CORE, columns), jnp.float32),
        ),
        query_in[0, 0], query_out[0, 0], in_basis, out_basis, eigen_values[0], mine,
    )
    partial_theirs = scores_of(theirs, preconds, length, columns)
    partial_value = partial_mine + partial_theirs

    k = jnp.arange(X * CORE, dtype=jnp.int32)
    owner = (lax.axis_index("x") ^ (k % X)) * CORE + (lax.axis_index("core") ^ (k // X))
    order = owner[None, :] == k[:, None]
    ordered = jnp.sum(
        jnp.where(order[:, :, None], partial_value[None, :, :], 0.0), axis=1
    )
    spread = jnp.broadcast_to(ordered[None], (Y,) + ordered.shape).reshape(Y * X * CORE, -1)
    near = jnp.sum(lax.all_to_all(spread, ("y", "x", "core"), 0, 0), axis=0)
    far = jnp.broadcast_to(near[None], (ZLO,) + near.shape)
    summed = jnp.sum(lax.all_to_all(far, "zlo", 0, 0), axis=0)
    factor = 1.0 / math.sqrt(ZLO * Y * in_basis.shape[0] * out_basis.shape[0])
    scores = (summed * factor)[None, :]
    seat = jnp.arange(columns, dtype=jnp.int32)
    return jnp.where(query_ids[:, None] == seat[None, :], 0.0, scores)


def solution(mesh):
    split = Mesh(mesh.devices.reshape(ZLO, Y, ZHI, X, CORE), NAMES)
    layer, blk = ("zlo", "y"), ("zhi", "x", "core")
    placed = (
        P(layer, blk, None, None),
        P(layer, blk, None, None),
        P(layer, blk, None, None),
        P(layer, blk, None, None),
        P(layer, None, None),
        P(layer, None, None),
        P(layer, None, None),
        P(blk),
        P(blk),
    )
    return jax.shard_map(
        local, mesh=split, in_specs=placed, out_specs=P(blk, None), check_vma=False
    )
```

```python
import math

import jax
import jax.numpy as jnp
from jax import lax
from jax.experimental import pallas as pl
from jax.experimental.pallas import tpu as pltpu
from jax.sharding import Mesh
from jax.sharding import PartitionSpec as P

damping = 0.1

ZLO, Y, ZHI, X, CORE = 16, 4, 2, 4, 2
NAMES = ("zlo", "y", "zhi", "x", "core")
SWAP = [(0, 1), (1, 0)]
EXTRA = 8

VMEM = pl.BlockSpec(memory_space=pltpu.VMEM)
SMEM = pl.BlockSpec(memory_space=pltpu.SMEM)


def project(rows, basis):
    return jnp.dot(rows, basis, preferred_element_type=jnp.float32).astype(jnp.bfloat16)


def train_kernel(ids_ref, in_ref, out_ref, in_basis_ref, out_basis_ref, packed_ref):
    tokens = in_ref.shape[0]
    packed_ref[:tokens] = project(in_ref[...].astype(jnp.bfloat16), in_basis_ref[...])
    packed_ref[tokens : 2 * tokens] = project(out_ref[...].astype(jnp.bfloat16), out_basis_ref[...])
    row = lax.broadcasted_iota(jnp.int32, (EXTRA, in_ref.shape[1]), 0)
    lane = lax.broadcasted_iota(jnp.int32, (EXTRA, in_ref.shape[1]), 1)
    hit = (row == 0) & (lane == ids_ref[0])
    for s in range(1, ids_ref.shape[0]):
        hit = hit | ((row == s) & (lane == ids_ref[s]))
    packed_ref[2 * tokens :] = jnp.where(hit, 1.0, 0.0).astype(jnp.bfloat16)


def pack_train(train_ids, train_in, train_out, in_basis, out_basis):
    tokens, width = train_in.shape
    return pl.pallas_call(
        train_kernel,
        out_shape=jax.ShapeDtypeStruct((2 * tokens + EXTRA, width), jnp.bfloat16),
        in_specs=[SMEM] + [VMEM] * 4,
        out_specs=VMEM,
    )(train_ids, train_in, train_out, in_basis, out_basis)


def score_kernel(mine_ref, theirs_ref, here_ref, there_ref, out_ref, sums_ref, *, length, columns):
    step, steps = pl.program_id(0), pl.num_programs(0)
    tokens = (mine_ref.shape[0] - EXTRA) // 2
    seqs = tokens // length
    for p, packed_ref in enumerate((mine_ref, theirs_ref)):
        inside = packed_ref[:tokens].astype(jnp.float32)
        outside = packed_ref[tokens : 2 * tokens]
        for c, ref in enumerate((here_ref, there_ref)):
            prod = inside * jnp.dot(outside, ref[0], preferred_element_type=jnp.float32)
            for s in range(seqs):
                part = jnp.sum(prod[s * length : (s + 1) * length], axis=0, keepdims=True)
                sums_ref[p * seqs + s, pl.ds(c * X + step, 1), :] = part

    @pl.when(step == steps - 1)
    def _():
        total = jnp.zeros(out_ref.shape, jnp.float32)
        for p, packed_ref in enumerate((mine_ref, theirs_ref)):
            hot = packed_ref[2 * tokens :].astype(jnp.float32)
            for s in range(seqs):
                sums = jnp.sum(sums_ref[p * seqs + s], axis=1, keepdims=True)
                total = total + sums * hot[s : s + 1, :columns]
        out_ref[...] = total


def scores_of(mine, theirs, here, there, length, columns):
    queries, rows, width = here.shape
    seqs = (mine.shape[0] - EXTRA) // 2 // length
    each = pl.BlockSpec((1, rows, width), lambda i: (i, 0, 0))
    return pl.pallas_call(
        lambda *refs: score_kernel(*refs, length=length, columns=columns),
        out_shape=jax.ShapeDtypeStruct((CORE * queries, columns), jnp.float32),
        grid=(queries,),
        in_specs=[VMEM, VMEM, each, each],
        out_specs=pl.BlockSpec((CORE * queries, columns), lambda i: (0, 0)),
        scratch_shapes=[pltpu.VMEM((2 * seqs, CORE * queries, width), jnp.float32)],
    )(mine, theirs, here, there)


def gather_preconds(query_in, query_out, in_basis, out_basis, eigen_values):
    side_in = project(query_in, in_basis)
    side_out = project(query_out, out_basis)
    moment = lax.dot_general(
        side_out, side_in, (((0,), (0,)), ((), ())), preferred_element_type=jnp.float32
    )
    scale = query_in.shape[0] * (eigen_values + damping)
    precond = (moment / scale).astype(jnp.bfloat16)
    along = [precond]
    for step in range(1, X):
        along.append(lax.ppermute(precond, "x", [(i, i ^ step) for i in range(X)]))
    here = jnp.stack(along)
    return [here, lax.ppermute(here, "core", SWAP)]


def local(
    train_in,
    train_out,
    query_in,
    query_out,
    basis_in,
    basis_out,
    eigen_values,
    train_ids,
    query_ids,
):
    in_basis = basis_in[0]
    out_basis = basis_out[0]
    seqs, length, width = train_in.shape[1:]
    columns = seqs * ZHI * X * CORE
    tokens = (seqs * length, width)

    mine = pack_train(
        train_ids, train_in[0].reshape(tokens), train_out[0].reshape(tokens), in_basis, out_basis
    )
    theirs = lax.ppermute(mine, "zhi", SWAP)
    here, there = lax.cond(
        lax.axis_index("x") < X,
        gather_preconds,
        lambda *ops: [jnp.zeros((X, width, width), jnp.bfloat16)] * CORE,
        query_in[0, 0], query_out[0, 0], in_basis, out_basis, eigen_values[0],
    )
    partial_value = scores_of(mine, theirs, here, there, length, columns)

    k = jnp.arange(X * CORE, dtype=jnp.int32)
    owner = (lax.axis_index("x") ^ (k % X)) * CORE + (lax.axis_index("core") ^ (k // X))
    order = owner[None, :] == k[:, None]
    ordered = jnp.sum(
        jnp.where(order[:, :, None], partial_value[None, :, :], 0.0), axis=1
    )
    spread = jnp.broadcast_to(ordered[None], (Y,) + ordered.shape).reshape(Y * X * CORE, -1)
    near = jnp.sum(lax.all_to_all(spread, ("y", "x", "core"), 0, 0), axis=0)
    far = jnp.broadcast_to(near[None], (ZLO,) + near.shape)
    summed = jnp.sum(lax.all_to_all(far, "zlo", 0, 0), axis=0)
    factor = 1.0 / math.sqrt(ZLO * Y * in_basis.shape[0] * out_basis.shape[0])
    scores = (summed * factor)[None, :]
    seat = jnp.arange(columns, dtype=jnp.int32)
    return jnp.where(query_ids[:, None] == seat[None, :], 0.0, scores)


def solution(mesh):
    split = Mesh(mesh.devices.reshape(ZLO, Y, ZHI, X, CORE), NAMES)
    layer, blk = ("zlo", "y"), ("zhi", "x", "core")
    placed = (
        P(layer, blk, None, None),
        P(layer, blk, None, None),
        P(layer, blk, None, None),
        P(layer, blk, None, None),
        P(layer, None, None),
        P(layer, None, None),
        P(layer, None, None),
        P(blk),
        P(blk),
    )
    return jax.shard_map(
        local, mesh=split, in_specs=placed, out_specs=P(blk, None), check_vma=False
    )
```

```python
import math

import jax
import jax.numpy as jnp
from jax import lax
from jax.experimental import pallas as pl
from jax.experimental.pallas import tpu as pltpu
from jax.sharding import Mesh
from jax.sharding import PartitionSpec as P

damping = 0.1

ZLO, Y, ZHI, X, CORE = 16, 4, 2, 4, 2
NAMES = ("zlo", "y", "zhi", "x", "core")
SWAP = [(0, 1), (1, 0)]
EXTRA = 8

VMEM = pl.BlockSpec(memory_space=pltpu.VMEM)
SMEM = pl.BlockSpec(memory_space=pltpu.SMEM)


def project(rows, basis):
    return jnp.dot(rows, basis, preferred_element_type=jnp.float32).astype(jnp.bfloat16)


def train_kernel(ids_ref, in_ref, out_ref, in_basis_ref, out_basis_ref, packed_ref):
    tokens = in_ref.shape[0]
    packed_ref[:tokens] = project(in_ref[...].astype(jnp.bfloat16), in_basis_ref[...])
    packed_ref[tokens : 2 * tokens] = project(out_ref[...].astype(jnp.bfloat16), out_basis_ref[...])
    row = lax.broadcasted_iota(jnp.int32, (EXTRA, in_ref.shape[1]), 0)
    lane = lax.broadcasted_iota(jnp.int32, (EXTRA, in_ref.shape[1]), 1)
    hit = (row == 0) & (lane == ids_ref[0])
    for s in range(1, ids_ref.shape[0]):
        hit = hit | ((row == s) & (lane == ids_ref[s]))
    packed_ref[2 * tokens :] = jnp.where(hit, 1.0, 0.0).astype(jnp.bfloat16)


def pack_train(train_ids, train_in, train_out, in_basis, out_basis):
    tokens, width = train_in.shape
    return pl.pallas_call(
        train_kernel,
        out_shape=jax.ShapeDtypeStruct((2 * tokens + EXTRA, width), jnp.bfloat16),
        in_specs=[SMEM] + [VMEM] * 4,
        out_specs=VMEM,
    )(train_ids, train_in, train_out, in_basis, out_basis)


def score_kernel(*refs, length, columns):
    packed_refs, precond_refs, out_ref = refs[:4], refs[4:-1], refs[-1]
    tokens = (packed_refs[0].shape[0] - EXTRA) // 2
    seqs = tokens // length
    total = None
    for packed_ref in packed_refs:
        inside = packed_ref[:tokens].astype(jnp.float32)
        outside = packed_ref[tokens : 2 * tokens]
        hot = packed_ref[2 * tokens :].astype(jnp.float32)
        rows = [[] for _ in range(seqs)]
        for ref in precond_refs:
            prod = inside * jnp.dot(outside, ref[...], preferred_element_type=jnp.float32)
            for s in range(seqs):
                part = prod[s * length : (s + 1) * length]
                rows[s].append(jnp.sum(part, axis=0, keepdims=True))
        for s in range(seqs):
            sums = jnp.sum(jnp.concatenate(rows[s], axis=0), axis=1, keepdims=True)
            placed = sums * hot[s : s + 1, :columns]
            total = placed if total is None else total + placed
    out_ref[...] = total


def scores_of(packed, preconds, length, columns):
    return pl.pallas_call(
        lambda *refs: score_kernel(*refs, length=length, columns=columns),
        out_shape=jax.ShapeDtypeStruct((len(preconds), columns), jnp.float32),
        in_specs=[VMEM] * (len(packed) + len(preconds)),
        out_specs=VMEM,
        compiler_params=pltpu.CompilerParams(vmem_limit_bytes=40 << 20),
    )(*packed, *preconds)


def precondition(query_in, query_out, in_basis, out_basis, eigen_values):
    side_in = project(query_in, in_basis)
    side_out = project(query_out, out_basis)
    moment = lax.dot_general(
        side_out, side_in, (((0,), (0,)), ((), ())), preferred_element_type=jnp.float32
    )
    scale = query_in.shape[0] * (eigen_values + damping)
    return (moment / scale).astype(jnp.bfloat16)


def local(
    train_in,
    train_out,
    query_in,
    query_out,
    basis_in,
    basis_out,
    eigen_values,
    train_ids,
    query_ids,
):
    in_basis = basis_in[0]
    out_basis = basis_out[0]
    seqs, length, width = train_in.shape[1:]
    columns = seqs * ZHI * X * CORE
    tokens = (seqs * length, width)

    mine = pack_train(
        train_ids, train_in[0].reshape(tokens), train_out[0].reshape(tokens), in_basis, out_basis
    )
    theirs = lax.ppermute(mine, "zhi", SWAP)
    packed = [mine, lax.ppermute(mine, "core", SWAP), theirs, lax.ppermute(theirs, "core", SWAP)]
    precond = precondition(query_in[0, 0], query_out[0, 0], in_basis, out_basis, eigen_values[0])
    preconds = [precond]
    for step in range(1, X):
        preconds.append(lax.ppermute(precond, "x", [(i, i ^ step) for i in range(X)]))
    partial_value = scores_of(packed, preconds, length, columns)

    k = jnp.arange(X, dtype=jnp.int32)
    order = (lax.axis_index("x") ^ k)[None, :] == k[:, None]
    ordered = jnp.sum(
        jnp.where(order[:, :, None], partial_value[None, :, :], 0.0), axis=1
    )
    spread = jnp.broadcast_to(ordered[None], (Y,) + ordered.shape).reshape(Y * X, -1)
    near = jnp.sum(lax.all_to_all(spread, ("y", "x"), 0, 0), axis=0)
    far = jnp.broadcast_to(near[None], (ZLO,) + near.shape)
    summed = jnp.sum(lax.all_to_all(far, "zlo", 0, 0), axis=0)
    factor = 1.0 / math.sqrt(ZLO * Y * in_basis.shape[0] * out_basis.shape[0])
    scores = (summed * factor)[None, :]
    seat = jnp.arange(columns, dtype=jnp.int32)
    return jnp.where(query_ids[:, None] == seat[None, :], 0.0, scores)


def solution(mesh):
    split = Mesh(mesh.devices.reshape(ZLO, Y, ZHI, X, CORE), NAMES)
    layer, blk = ("zlo", "y"), ("zhi", "x", "core")
    placed = (
        P(layer, blk, None, None),
        P(layer, blk, None, None),
        P(layer, blk, None, None),
        P(layer, blk, None, None),
        P(layer, None, None),
        P(layer, None, None),
        P(layer, None, None),
        P(blk),
        P(blk),
    )
    return jax.shard_map(
        local, mesh=split, in_specs=placed, out_specs=P(blk, None), check_vma=False
    )
```

```python
import math

import jax
import jax.numpy as jnp
from jax import lax
from jax.experimental import pallas as pl
from jax.experimental.pallas import tpu as pltpu
from jax.sharding import Mesh
from jax.sharding import PartitionSpec as P

damping = 0.1

ZLO, Y, ZHI, X, CORE = 16, 4, 2, 4, 2
NAMES = ("zlo", "y", "zhi", "x", "core")
SWAP = [(0, 1), (1, 0)]
LANES = 128
EXTRA = 8

VMEM = pl.BlockSpec(memory_space=pltpu.VMEM)
SMEM = pl.BlockSpec(memory_space=pltpu.SMEM)


def project(rows, basis):
    return jnp.dot(rows, basis, preferred_element_type=jnp.float32).astype(jnp.bfloat16)


def train_kernel(ids_ref, in_ref, out_ref, in_basis_ref, out_basis_ref, packed_ref):
    tokens, width = in_ref.shape
    inside = project(in_ref[...].astype(jnp.bfloat16), in_basis_ref[...])
    outside = project(out_ref[...].astype(jnp.bfloat16), out_basis_ref[...])
    for at, side in ((0, inside), (width // LANES, outside)):
        for c in range(width // LANES):
            packed_ref[(at + c) * tokens : (at + c + 1) * tokens] = side[:, c * LANES : (c + 1) * LANES]
    row = lax.broadcasted_iota(jnp.int32, (EXTRA, LANES), 0)
    lane = lax.broadcasted_iota(jnp.int32, (EXTRA, LANES), 1)
    hit = (row == 0) & (lane == ids_ref[0])
    for s in range(1, ids_ref.shape[0]):
        hit = hit | ((row == s) & (lane == ids_ref[s]))
    packed_ref[packed_ref.shape[0] - EXTRA :] = jnp.where(hit, 1.0, 0.0).astype(jnp.bfloat16)


def pack_train(train_ids, train_in, train_out, in_basis, out_basis):
    tokens, width = train_in.shape
    return pl.pallas_call(
        train_kernel,
        out_shape=jax.ShapeDtypeStruct((2 * tokens * width // LANES + EXTRA, LANES), jnp.bfloat16),
        in_specs=[SMEM] + [VMEM] * 4,
        out_specs=VMEM,
    )(train_ids, train_in, train_out, in_basis, out_basis)


def packed_scores(packed_ref, preconds, length, columns):
    end = packed_ref.shape[0] - EXTRA
    tokens = end * LANES // (2 * preconds[0].shape[0])
    seqs = tokens // length
    blocks = [packed_ref[at : at + tokens] for at in range(0, end, tokens)]
    inside = jnp.concatenate(blocks[: len(blocks) // 2], axis=1).astype(jnp.float32)
    outside = jnp.concatenate(blocks[len(blocks) // 2 :], axis=1)
    hot = packed_ref[end:].astype(jnp.float32)
    rows = [[] for _ in range(seqs)]
    for precond in preconds:
        prod = inside * jnp.dot(outside, precond[...], preferred_element_type=jnp.float32)
        for s in range(seqs):
            rows[s].append(jnp.sum(prod[s * length : (s + 1) * length], axis=0, keepdims=True))
    total = None
    for s in range(seqs):
        sums = jnp.sum(jnp.concatenate(rows[s], axis=0), axis=1, keepdims=True)
        placed = sums * hot[s : s + 1, :columns]
        total = placed if total is None else total + placed
    return total


def first_scores(packed, preconds, length, columns):
    count = len(preconds)

    def kernel(packed_ref, *refs):
        stack_ref, out_ref = refs[-2:]
        out_ref[...] = packed_scores(packed_ref, refs[:count], length, columns)
        for q in range(count):
            stack_ref[q] = refs[q][...]

    return pl.pallas_call(
        kernel,
        out_shape=[
            jax.ShapeDtypeStruct((count,) + preconds[0].shape, jnp.bfloat16),
            jax.ShapeDtypeStruct((count, columns), jnp.float32),
        ],
        in_specs=[VMEM] * (1 + count),
        out_specs=[VMEM] * 2,
        compiler_params=pltpu.CompilerParams(vmem_limit_bytes=40 << 20),
    )(packed, *preconds)


def last_scores(packed, stack, before, length, columns):
    def kernel(packed_ref, stack_ref, before_ref, out_ref):
        preconds = [stack_ref.at[q] for q in range(stack_ref.shape[0])]
        out_ref[...] = before_ref[...] + packed_scores(packed_ref, preconds, length, columns)

    return pl.pallas_call(
        kernel,
        out_shape=jax.ShapeDtypeStruct(before.shape, jnp.float32),
        in_specs=[VMEM] * 3,
        out_specs=VMEM,
        compiler_params=pltpu.CompilerParams(vmem_limit_bytes=40 << 20),
    )(packed, stack, before)


def gather_preconds(query_in, query_out, in_basis, out_basis, eigen_values):
    side_in = project(query_in, in_basis)
    side_out = project(query_out, out_basis)
    moment = lax.dot_general(
        side_out, side_in, (((0,), (0,)), ((), ())), preferred_element_type=jnp.float32
    )
    scale = query_in.shape[0] * (eigen_values + damping)
    precond = (moment / scale).astype(jnp.bfloat16)
    along = [precond]
    for step in range(1, X):
        along.append(lax.ppermute(precond, "x", [(i, i ^ step) for i in range(X)]))
    beside = [lax.ppermute(p, "core", SWAP) for p in along]
    return along + beside


def local(
    train_in,
    train_out,
    query_in,
    query_out,
    basis_in,
    basis_out,
    eigen_values,
    train_ids,
    query_ids,
):
    in_basis = basis_in[0]
    out_basis = basis_out[0]
    seqs, length, width = train_in.shape[1:]
    columns = seqs * ZHI * X * CORE
    tokens = (seqs * length, width)

    mine = pack_train(
        train_ids, train_in[0].reshape(tokens), train_out[0].reshape(tokens), in_basis, out_basis
    )
    theirs = lax.ppermute(mine, "zhi", SWAP)
    preconds = lax.cond(
        lax.axis_index("x") < X,
        gather_preconds,
        lambda *ops: [jnp.zeros((width, width), jnp.bfloat16)] * (X * CORE),
        query_in[0, 0], query_out[0, 0], in_basis, out_basis, eigen_values[0],
    )
    stack, partial_mine = first_scores(mine, preconds, length, columns)
    partial_value = last_scores(theirs, stack, partial_mine, length, columns)

    k = jnp.arange(X * CORE, dtype=jnp.int32)
    owner = (lax.axis_index("x") ^ (k % X)) * CORE + (lax.axis_index("core") ^ (k // X))
    order = owner[None, :] == k[:, None]
    ordered = jnp.sum(
        jnp.where(order[:, :, None], partial_value[None, :, :], 0.0), axis=1
    )
    spread = jnp.broadcast_to(ordered[None], (Y,) + ordered.shape).reshape(Y * X * CORE, -1)
    near = jnp.sum(lax.all_to_all(spread, ("y", "x", "core"), 0, 0), axis=0)
    far = jnp.broadcast_to(near[None], (ZLO,) + near.shape)
    summed = jnp.sum(lax.all_to_all(far, "zlo", 0, 0), axis=0)
    factor = 1.0 / math.sqrt(ZLO * Y * in_basis.shape[0] * out_basis.shape[0])
    scores = (summed * factor)[None, :]
    seat = jnp.arange(columns, dtype=jnp.int32)
    return jnp.where(query_ids[:, None] == seat[None, :], 0.0, scores)


def solution(mesh):
    split = Mesh(mesh.devices.reshape(ZLO, Y, ZHI, X, CORE), NAMES)
    layer, blk = ("zlo", "y"), ("zhi", "x", "core")
    placed = (
        P(layer, blk, None, None),
        P(layer, blk, None, None),
        P(layer, blk, None, None),
        P(layer, blk, None, None),
        P(layer, None, None),
        P(layer, None, None),
        P(layer, None, None),
        P(blk),
        P(blk),
    )
    return jax.shard_map(
        local, mesh=split, in_specs=placed, out_specs=P(blk, None), check_vma=False
    )
```

```python
import math

import jax
import jax.numpy as jnp
from jax import lax
from jax.experimental import pallas as pl
from jax.experimental.pallas import tpu as pltpu
from jax.sharding import Mesh
from jax.sharding import PartitionSpec as P

damping = 0.1

ZLO, Y, ZHI, X, CORE = 16, 4, 2, 4, 2
NAMES = ("zlo", "y", "zhi", "x", "core")
SWAP = [(0, 1), (1, 0)]
LANES = 128
EXTRA = 8

VMEM = pl.BlockSpec(memory_space=pltpu.VMEM)
SMEM = pl.BlockSpec(memory_space=pltpu.SMEM)


def project(rows, basis):
    return jnp.dot(rows, basis, preferred_element_type=jnp.float32).astype(jnp.bfloat16)


def train_kernel(
    ids_ref, in_ref, out_ref, in_basis_ref, out_basis_ref, packed_ref,
    tokens_vmem, basis_vmem, packed_vmem, read, write,
):
    tokens, width = in_ref.shape
    sides = ((in_ref, in_basis_ref), (out_ref, out_basis_ref))
    reads = []
    for k, refs in enumerate(sides):
        for n, (ref, vmem) in enumerate(zip(refs, (tokens_vmem, basis_vmem))):
            reads.append(pltpu.make_async_copy(ref, vmem.at[k], read.at[2 * k + n]))
            reads[-1].start()
    row = lax.broadcasted_iota(jnp.int32, (EXTRA, LANES), 0)
    lane = lax.broadcasted_iota(jnp.int32, (EXTRA, LANES), 1)
    hit = (row == 0) & (lane == ids_ref[0])
    for s in range(1, ids_ref.shape[0]):
        hit = hit | ((row == s) & (lane == ids_ref[s]))
    size = tokens * width // LANES
    packed_vmem[2 * size :] = jnp.where(hit, 1.0, 0.0).astype(jnp.bfloat16)
    writes = []
    for k in range(len(sides)):
        reads[2 * k].wait()
        reads[2 * k + 1].wait()
        side = project(tokens_vmem[k].astype(jnp.bfloat16), basis_vmem[k])
        for c in range(width // LANES):
            start = k * size + c * tokens
            packed_vmem[start : start + tokens] = side[:, c * LANES : (c + 1) * LANES]
        part = pl.ds(k * size, size + (EXTRA if k else 0))
        writes.append(pltpu.make_async_copy(packed_vmem.at[part], packed_ref.at[part], write.at[k]))
        writes[-1].start()
    for copy in writes:
        copy.wait()


def pack_train(train_ids, train_in, train_out, in_basis, out_basis):
    tokens, width = train_in.shape
    packed = (2 * tokens * width // LANES + EXTRA, LANES)
    anywhere = pl.BlockSpec(memory_space=pl.ANY)
    return pl.pallas_call(
        train_kernel,
        out_shape=jax.ShapeDtypeStruct(packed, jnp.bfloat16),
        in_specs=[SMEM] + [anywhere] * 4,
        out_specs=anywhere,
        scratch_shapes=[
            pltpu.VMEM((2, tokens, width), jnp.float32),
            pltpu.VMEM((2, width, width), jnp.bfloat16),
            pltpu.VMEM(packed, jnp.bfloat16),
            pltpu.SemaphoreType.DMA((4,)),
            pltpu.SemaphoreType.DMA((2,)),
        ],
    )(train_ids, train_in, train_out, in_basis, out_basis)


def packed_scores(packed_ref, preconds, length, columns):
    end = packed_ref.shape[0] - EXTRA
    tokens = end * LANES // (2 * preconds[0].shape[0])
    seqs = tokens // length
    blocks = [packed_ref[at : at + tokens] for at in range(0, end, tokens)]
    inside = jnp.concatenate(blocks[: len(blocks) // 2], axis=1).astype(jnp.float32)
    outside = jnp.concatenate(blocks[len(blocks) // 2 :], axis=1)
    hot = packed_ref[end:].astype(jnp.float32)
    rows = [[] for _ in range(seqs)]
    for precond in preconds:
        prod = inside * jnp.dot(outside, precond[...], preferred_element_type=jnp.float32)
        for s in range(seqs):
            rows[s].append(jnp.sum(prod[s * length : (s + 1) * length], axis=0, keepdims=True))
    total = None
    for s in range(seqs):
        sums = jnp.sum(jnp.concatenate(rows[s], axis=0), axis=1, keepdims=True)
        placed = sums * hot[s : s + 1, :columns]
        total = placed if total is None else total + placed
    return total


def first_scores(packed, preconds, length, columns):
    count = len(preconds)

    def kernel(packed_ref, *refs):
        stack_ref, out_ref = refs[-2:]
        out_ref[...] = packed_scores(packed_ref, refs[:count], length, columns)
        for q in range(count):
            stack_ref[q] = refs[q][...]

    return pl.pallas_call(
        kernel,
        out_shape=[
            jax.ShapeDtypeStruct((count,) + preconds[0].shape, jnp.bfloat16),
            jax.ShapeDtypeStruct((count, columns), jnp.float32),
        ],
        in_specs=[VMEM] * (1 + count),
        out_specs=[VMEM] * 2,
        compiler_params=pltpu.CompilerParams(vmem_limit_bytes=40 << 20),
    )(packed, *preconds)


def last_scores(packed, stack, before, length, columns):
    def kernel(packed_ref, stack_ref, before_ref, out_ref):
        preconds = [stack_ref.at[q] for q in range(stack_ref.shape[0])]
        out_ref[...] = before_ref[...] + packed_scores(packed_ref, preconds, length, columns)

    return pl.pallas_call(
        kernel,
        out_shape=jax.ShapeDtypeStruct(before.shape, jnp.float32),
        in_specs=[VMEM] * 3,
        out_specs=VMEM,
        compiler_params=pltpu.CompilerParams(vmem_limit_bytes=40 << 20),
    )(packed, stack, before)


def precondition(query_in, query_out, in_basis, out_basis, eigen_values):
    side_in = project(query_in, in_basis)
    side_out = project(query_out, out_basis)
    moment = lax.dot_general(
        side_out, side_in, (((0,), (0,)), ((), ())), preferred_element_type=jnp.float32
    )
    scale = query_in.shape[0] * (eigen_values + damping)
    return (moment / scale).astype(jnp.bfloat16)


def gather_preconds(precond):
    along = [precond]
    for step in range(1, X):
        along.append(lax.ppermute(precond, "x", [(i, i ^ step) for i in range(X)]))
    beside = [lax.ppermute(p, "core", SWAP) for p in along]
    return along + beside


def local(
    train_in,
    train_out,
    query_in,
    query_out,
    basis_in,
    basis_out,
    eigen_values,
    train_ids,
    query_ids,
):
    in_basis = basis_in[0]
    out_basis = basis_out[0]
    seqs, length, width = train_in.shape[1:]
    columns = seqs * ZHI * X * CORE
    tokens = (seqs * length, width)

    mine = pack_train(
        train_ids, train_in[0].reshape(tokens), train_out[0].reshape(tokens), in_basis, out_basis
    )
    theirs = lax.ppermute(mine, "zhi", SWAP)
    precond = precondition(query_in[0, 0], query_out[0, 0], in_basis, out_basis, eigen_values[0])
    preconds = lax.cond(
        lax.axis_index("x") < X, gather_preconds, lambda precond: [precond] * (X * CORE), precond
    )
    stack, partial_mine = first_scores(mine, preconds, length, columns)
    partial_value = last_scores(theirs, stack, partial_mine, length, columns)

    k = jnp.arange(X * CORE, dtype=jnp.int32)
    owner = (lax.axis_index("x") ^ (k % X)) * CORE + (lax.axis_index("core") ^ (k // X))
    order = owner[None, :] == k[:, None]
    ordered = jnp.sum(
        jnp.where(order[:, :, None], partial_value[None, :, :], 0.0), axis=1
    )
    spread = jnp.broadcast_to(ordered[None], (Y,) + ordered.shape).reshape(Y * X * CORE, -1)
    near = jnp.sum(lax.all_to_all(spread, ("y", "x", "core"), 0, 0), axis=0)
    far = jnp.broadcast_to(near[None], (ZLO,) + near.shape)
    summed = jnp.sum(lax.all_to_all(far, "zlo", 0, 0), axis=0)
    factor = 1.0 / math.sqrt(ZLO * Y * in_basis.shape[0] * out_basis.shape[0])
    scores = (summed * factor)[None, :]
    seat = jnp.arange(columns, dtype=jnp.int32)
    return jnp.where(query_ids[:, None] == seat[None, :], 0.0, scores)


def solution(mesh):
    split = Mesh(mesh.devices.reshape(ZLO, Y, ZHI, X, CORE), NAMES)
    layer, blk = ("zlo", "y"), ("zhi", "x", "core")
    placed = (
        P(layer, blk, None, None),
        P(layer, blk, None, None),
        P(layer, blk, None, None),
        P(layer, blk, None, None),
        P(layer, None, None),
        P(layer, None, None),
        P(layer, None, None),
        P(blk),
        P(blk),
    )
    return jax.shard_map(
        local, mesh=split, in_specs=placed, out_specs=P(blk, None), check_vma=False
    )
```

```python
import math

import jax
import jax.numpy as jnp
from jax import lax
from jax.experimental import pallas as pl
from jax.experimental.pallas import tpu as pltpu
from jax.sharding import Mesh
from jax.sharding import PartitionSpec as P

damping = 0.1

ZLO, Y, ZHI, X, CORE = 16, 4, 2, 4, 2
NAMES = ("zlo", "y", "zhi", "x", "core")
SWAP = [(0, 1), (1, 0)]
LANES = 128
EXTRA = 8

VMEM = pl.BlockSpec(memory_space=pltpu.VMEM)
SMEM = pl.BlockSpec(memory_space=pltpu.SMEM)


def project(rows, basis):
    return jnp.dot(rows, basis, preferred_element_type=jnp.float32).astype(jnp.bfloat16)


def train_kernel(ids_ref, in_ref, out_ref, in_basis_ref, out_basis_ref, packed_ref):
    tokens, width = in_ref.shape
    inside = project(in_ref[...].astype(jnp.bfloat16), in_basis_ref[...])
    outside = project(out_ref[...].astype(jnp.bfloat16), out_basis_ref[...])
    for at, side in ((0, inside), (width // LANES, outside)):
        for c in range(width // LANES):
            packed_ref[(at + c) * tokens : (at + c + 1) * tokens] = side[:, c * LANES : (c + 1) * LANES]
    row = lax.broadcasted_iota(jnp.int32, (EXTRA, LANES), 0)
    lane = lax.broadcasted_iota(jnp.int32, (EXTRA, LANES), 1)
    hit = (row == 0) & (lane == ids_ref[0])
    for s in range(1, ids_ref.shape[0]):
        hit = hit | ((row == s) & (lane == ids_ref[s]))
    packed_ref[packed_ref.shape[0] - EXTRA :] = jnp.where(hit, 1.0, 0.0).astype(jnp.bfloat16)


def pack_train(train_ids, train_in, train_out, in_basis, out_basis):
    tokens, width = train_in.shape
    return pl.pallas_call(
        train_kernel,
        out_shape=jax.ShapeDtypeStruct((2 * tokens * width // LANES + EXTRA, LANES), jnp.bfloat16),
        in_specs=[SMEM] + [VMEM] * 4,
        out_specs=VMEM,
    )(train_ids, train_in, train_out, in_basis, out_basis)


def packed_scores(packed_ref, preconds, length, columns):
    end = packed_ref.shape[0] - EXTRA
    tokens = end * LANES // (2 * preconds[0].shape[0])
    seqs = tokens // length
    blocks = [packed_ref[at : at + tokens] for at in range(0, end, tokens)]
    inside = jnp.concatenate(blocks[: len(blocks) // 2], axis=1).astype(jnp.float32)
    outside = jnp.concatenate(blocks[len(blocks) // 2 :], axis=1)
    hot = packed_ref[end:].astype(jnp.float32)
    rows = [[] for _ in range(seqs)]
    for precond in preconds:
        prod = inside * jnp.dot(outside, precond[...], preferred_element_type=jnp.float32)
        for s in range(seqs):
            rows[s].append(jnp.sum(prod[s * length : (s + 1) * length], axis=0, keepdims=True))
    total = None
    for s in range(seqs):
        sums = jnp.sum(jnp.concatenate(rows[s], axis=0), axis=1, keepdims=True)
        placed = sums * hot[s : s + 1, :columns]
        total = placed if total is None else total + placed
    return total


def first_scores(packed, preconds, length, columns):
    count = len(preconds)

    def kernel(packed_ref, *refs):
        stack_ref, out_ref = refs[-2:]
        out_ref[...] = packed_scores(packed_ref, refs[:count], length, columns)
        for q in range(count):
            stack_ref[q] = refs[q][...]

    return pl.pallas_call(
        kernel,
        out_shape=[
            jax.ShapeDtypeStruct((count,) + preconds[0].shape, jnp.bfloat16),
            jax.ShapeDtypeStruct((count, columns), jnp.float32),
        ],
        in_specs=[VMEM] * (1 + count),
        out_specs=[VMEM] * 2,
        compiler_params=pltpu.CompilerParams(vmem_limit_bytes=40 << 20),
    )(packed, *preconds)


def last_scores(late, early, stack, before, length, columns):
    def kernel(late_ref, early_ref, stack_ref, before_ref, out_ref, packed_ref):
        packed_ref[...] = late_ref[...] + early_ref[...]
        preconds = [stack_ref.at[q] for q in range(stack_ref.shape[0])]
        out_ref[...] = before_ref[...] + packed_scores(packed_ref, preconds, length, columns)

    return pl.pallas_call(
        kernel,
        out_shape=jax.ShapeDtypeStruct(before.shape, jnp.float32),
        in_specs=[VMEM] * 4,
        out_specs=VMEM,
        scratch_shapes=[pltpu.VMEM(late.shape, late.dtype)],
        compiler_params=pltpu.CompilerParams(vmem_limit_bytes=40 << 20),
    )(late, early, stack, before)


def precondition(query_in, query_out, in_basis, out_basis, eigen_values):
    side_in = project(query_in, in_basis)
    side_out = project(query_out, out_basis)
    moment = lax.dot_general(
        side_out, side_in, (((0,), (0,)), ((), ())), preferred_element_type=jnp.float32
    )
    scale = query_in.shape[0] * (eigen_values + damping)
    return (moment / scale).astype(jnp.bfloat16)


def gather_preconds(precond):
    one, two, three = [
        lax.ppermute(precond, "x", [(i, i ^ step) for i in range(X)]) for step in range(1, X)
    ]
    precond, one = lax.optimization_barrier((precond, one))
    other = lax.ppermute(precond, "core", SWAP)
    other, one, two = lax.optimization_barrier((other, one, two))
    return [precond, one, two, three, other] + [
        lax.ppermute(p, "core", SWAP) for p in (one, two, three)
    ]


def swap_half(packed, places):
    pairs = [(z * ZHI + i, z * ZHI + j) for z in places for i, j in SWAP]
    return lax.ppermute(packed, ("zlo", "zhi"), pairs)


def local(
    train_in,
    train_out,
    query_in,
    query_out,
    basis_in,
    basis_out,
    eigen_values,
    train_ids,
    query_ids,
):
    in_basis = basis_in[0]
    out_basis = basis_out[0]
    seqs, length, width = train_in.shape[1:]
    columns = seqs * ZHI * X * CORE
    tokens = (seqs * length, width)

    mine = pack_train(
        train_ids, train_in[0].reshape(tokens), train_out[0].reshape(tokens), in_basis, out_basis
    )
    late = swap_half(mine, range(ZLO // 2, ZLO))
    precond = precondition(query_in[0, 0], query_out[0, 0], in_basis, out_basis, eigen_values[0])
    again, precond = lax.optimization_barrier((mine, precond))
    early = swap_half(again, range(ZLO // 2))
    preconds = lax.cond(
        lax.axis_index("x") < X, gather_preconds, lambda precond: [precond] * (X * CORE), precond
    )
    stack, partial_mine = first_scores(mine, preconds, length, columns)
    partial_value = last_scores(late, early, stack, partial_mine, length, columns)

    k = jnp.arange(X * CORE, dtype=jnp.int32)
    owner = (lax.axis_index("x") ^ (k % X)) * CORE + (lax.axis_index("core") ^ (k // X))
    order = owner[None, :] == k[:, None]
    ordered = jnp.sum(
        jnp.where(order[:, :, None], partial_value[None, :, :], 0.0), axis=1
    )
    spread = jnp.broadcast_to(ordered[None], (Y,) + ordered.shape).reshape(Y * X * CORE, -1)
    near = jnp.sum(lax.all_to_all(spread, ("y", "x", "core"), 0, 0), axis=0)
    far = jnp.broadcast_to(near[None], (ZLO,) + near.shape)
    summed = jnp.sum(lax.all_to_all(far, "zlo", 0, 0), axis=0)
    factor = 1.0 / math.sqrt(ZLO * Y * in_basis.shape[0] * out_basis.shape[0])
    scores = (summed * factor)[None, :]
    seat = jnp.arange(columns, dtype=jnp.int32)
    return jnp.where(query_ids[:, None] == seat[None, :], 0.0, scores)


def solution(mesh):
    split = Mesh(mesh.devices.reshape(ZLO, Y, ZHI, X, CORE), NAMES)
    layer, blk = ("zlo", "y"), ("zhi", "x", "core")
    placed = (
        P(layer, blk, None, None),
        P(layer, blk, None, None),
        P(layer, blk, None, None),
        P(layer, blk, None, None),
        P(layer, None, None),
        P(layer, None, None),
        P(layer, None, None),
        P(blk),
        P(blk),
    )
    return jax.shard_map(
        local, mesh=split, in_specs=placed, out_specs=P(blk, None), check_vma=False
    )
```

```python
import math

import jax
import jax.numpy as jnp
from jax import lax
from jax.experimental import pallas as pl
from jax.experimental.pallas import tpu as pltpu
from jax.sharding import Mesh
from jax.sharding import PartitionSpec as P

damping = 0.1

ZLO, Y, ZHI, X, CORE = 16, 4, 2, 4, 2
NAMES = ("zlo", "y", "zhi", "x", "core")
SWAP = [(0, 1), (1, 0)]
LANES = 128
EXTRA = 8

VMEM = pl.BlockSpec(memory_space=pltpu.VMEM)
SMEM = pl.BlockSpec(memory_space=pltpu.SMEM)


def project(rows, basis):
    return jnp.dot(rows, basis, preferred_element_type=jnp.float32).astype(jnp.bfloat16)


def train_kernel(ids_ref, in_ref, out_ref, in_basis_ref, out_basis_ref, packed_ref):
    tokens, width = in_ref.shape
    inside = project(in_ref[...].astype(jnp.bfloat16), in_basis_ref[...])
    outside = project(out_ref[...].astype(jnp.bfloat16), out_basis_ref[...])
    for at, side in ((0, inside), (width // LANES, outside)):
        for c in range(width // LANES):
            packed_ref[(at + c) * tokens : (at + c + 1) * tokens] = side[:, c * LANES : (c + 1) * LANES]
    row = lax.broadcasted_iota(jnp.int32, (EXTRA, LANES), 0)
    lane = lax.broadcasted_iota(jnp.int32, (EXTRA, LANES), 1)
    hit = (row == 0) & (lane == ids_ref[0])
    for s in range(1, ids_ref.shape[0]):
        hit = hit | ((row == s) & (lane == ids_ref[s]))
    packed_ref[packed_ref.shape[0] - EXTRA :] = jnp.where(hit, 1.0, 0.0).astype(jnp.bfloat16)


def pack_train(train_ids, train_in, train_out, in_basis, out_basis):
    tokens, width = train_in.shape
    return pl.pallas_call(
        train_kernel,
        out_shape=jax.ShapeDtypeStruct((2 * tokens * width // LANES + EXTRA, LANES), jnp.bfloat16),
        in_specs=[SMEM] + [VMEM] * 4,
        out_specs=VMEM,
        cost_estimate=pl.CostEstimate(
            flops=400 * tokens * width * width, transcendentals=0, bytes_accessed=12 * tokens * width
        ),
    )(train_ids, train_in, train_out, in_basis, out_basis)


def packed_scores(packed_ref, preconds, length, columns):
    end = packed_ref.shape[0] - EXTRA
    tokens = end * LANES // (2 * preconds[0].shape[0])
    seqs = tokens // length
    blocks = [packed_ref[at : at + tokens] for at in range(0, end, tokens)]
    inside = jnp.concatenate(blocks[: len(blocks) // 2], axis=1).astype(jnp.float32)
    outside = jnp.concatenate(blocks[len(blocks) // 2 :], axis=1)
    hot = packed_ref[end:].astype(jnp.float32)
    rows = [[] for _ in range(seqs)]
    for precond in preconds:
        prod = inside * jnp.dot(outside, precond[...], preferred_element_type=jnp.float32)
        for s in range(seqs):
            rows[s].append(jnp.sum(prod[s * length : (s + 1) * length], axis=0, keepdims=True))
    total = None
    for s in range(seqs):
        sums = jnp.sum(jnp.concatenate(rows[s], axis=0), axis=1, keepdims=True)
        placed = sums * hot[s : s + 1, :columns]
        total = placed if total is None else total + placed
    return total


class Arriving:
    def __init__(self, ref, copy):
        self.ref, self.copy, self.shape = ref, copy, ref.shape

    def __getitem__(self, at):
        self.copy.wait()
        return self.ref[at]


def first_scores(packed, preconds, length, columns):
    count = len(preconds)

    def kernel(packed_ref, *refs):
        stack_ref, out_ref, sems = refs[-3:]
        copies = [
            pltpu.make_async_copy(refs[q], stack_ref.at[q], sems.at[q]) for q in range(count)
        ]
        for copy in copies:
            copy.start()
        arriving = [Arriving(stack_ref.at[q], copies[q]) for q in range(count)]
        out_ref[...] = packed_scores(packed_ref, arriving, length, columns)

    return pl.pallas_call(
        kernel,
        out_shape=[
            jax.ShapeDtypeStruct((count,) + preconds[0].shape, jnp.bfloat16),
            jax.ShapeDtypeStruct((count, columns), jnp.float32),
        ],
        in_specs=[VMEM] + [pl.BlockSpec(memory_space=pl.ANY)] * count,
        out_specs=[VMEM] * 2,
        scratch_shapes=[pltpu.SemaphoreType.DMA((count,))],
        compiler_params=pltpu.CompilerParams(vmem_limit_bytes=40 << 20),
    )(packed, *preconds)


def last_scores(late, early, stack, before, length, columns):
    def kernel(late_ref, early_ref, stack_ref, before_ref, out_ref, packed_ref):
        packed_ref[...] = late_ref[...] + early_ref[...]
        preconds = [stack_ref.at[q] for q in range(stack_ref.shape[0])]
        out_ref[...] = before_ref[...] + packed_scores(packed_ref, preconds, length, columns)

    return pl.pallas_call(
        kernel,
        out_shape=jax.ShapeDtypeStruct(before.shape, jnp.float32),
        in_specs=[VMEM] * 4,
        out_specs=VMEM,
        scratch_shapes=[pltpu.VMEM(late.shape, late.dtype)],
        compiler_params=pltpu.CompilerParams(vmem_limit_bytes=40 << 20),
    )(late, early, stack, before)


def precondition(query_in, query_out, in_basis, out_basis, eigen_values):
    side_in = project(query_in, in_basis)
    side_out = project(query_out, out_basis)
    moment = lax.dot_general(
        side_out, side_in, (((0,), (0,)), ((), ())), preferred_element_type=jnp.float32
    )
    scale = query_in.shape[0] * (eigen_values + damping)
    return (moment / scale).astype(jnp.bfloat16)


def gather_preconds(precond):
    one, two, three = [
        lax.ppermute(precond, "x", [(i, i ^ step) for i in range(X)]) for step in range(1, X)
    ]
    precond, one = lax.optimization_barrier((precond, one))
    other = lax.ppermute(precond, "core", SWAP)
    one, other = lax.optimization_barrier((one, other))
    return [precond, one, two, three, other] + [
        lax.ppermute(p, "core", SWAP) for p in (one, two, three)
    ]


def swap_half(packed, places):
    pairs = [(z * ZHI + i, z * ZHI + j) for z in places for i, j in SWAP]
    return lax.ppermute(packed, ("zlo", "zhi"), pairs)


def local(
    train_in,
    train_out,
    query_in,
    query_out,
    basis_in,
    basis_out,
    eigen_values,
    train_ids,
    query_ids,
):
    in_basis = basis_in[0]
    out_basis = basis_out[0]
    seqs, length, width = train_in.shape[1:]
    columns = seqs * ZHI * X * CORE
    tokens = (seqs * length, width)

    mine = pack_train(
        train_ids, train_in[0].reshape(tokens), train_out[0].reshape(tokens), in_basis, out_basis
    )
    late = swap_half(mine, range(ZLO // 2, ZLO))
    precond = precondition(query_in[0, 0], query_out[0, 0], in_basis, out_basis, eigen_values[0])
    again, precond = lax.optimization_barrier((mine, precond))
    early = swap_half(again, range(ZLO // 2))
    preconds = lax.cond(
        lax.axis_index("x") < X, gather_preconds, lambda precond: [precond] * (X * CORE), precond
    )
    stack, partial_mine = first_scores(mine, preconds, length, columns)
    partial_value = last_scores(late, early, stack, partial_mine, length, columns)

    k = jnp.arange(X * CORE, dtype=jnp.int32)
    owner = (lax.axis_index("x") ^ (k % X)) * CORE + (lax.axis_index("core") ^ (k // X))
    order = owner[None, :] == k[:, None]
    ordered = jnp.sum(
        jnp.where(order[:, :, None], partial_value[None, :, :], 0.0), axis=1
    )
    spread = jnp.broadcast_to(ordered[None], (Y,) + ordered.shape).reshape(Y * X * CORE, -1)
    near = jnp.sum(lax.all_to_all(spread, ("y", "x", "core"), 0, 0), axis=0)
    far = jnp.broadcast_to(near[None], (ZLO,) + near.shape)
    summed = jnp.sum(lax.all_to_all(far, "zlo", 0, 0), axis=0)
    factor = 1.0 / math.sqrt(ZLO * Y * in_basis.shape[0] * out_basis.shape[0])
    scores = (summed * factor)[None, :]
    seat = jnp.arange(columns, dtype=jnp.int32)
    return jnp.where(query_ids[:, None] == seat[None, :], 0.0, scores)


def solution(mesh):
    split = Mesh(mesh.devices.reshape(ZLO, Y, ZHI, X, CORE), NAMES)
    layer, blk = ("zlo", "y"), ("zhi", "x", "core")
    placed = (
        P(layer, blk, None, None),
        P(layer, blk, None, None),
        P(layer, blk, None, None),
        P(layer, blk, None, None),
        P(layer, None, None),
        P(layer, None, None),
        P(layer, None, None),
        P(blk),
        P(blk),
    )
    return jax.shard_map(
        local, mesh=split, in_specs=placed, out_specs=P(blk, None), check_vma=False
    )
```

```python
import math

import jax
import jax.numpy as jnp
from jax import lax
from jax.experimental import pallas as pl
from jax.experimental.pallas import tpu as pltpu
from jax.sharding import Mesh
from jax.sharding import PartitionSpec as P

damping = 0.1

ZLO, Y, ZHI, X, CORE = 16, 4, 2, 4, 2
NAMES = ("zlo", "y", "zhi", "x", "core")
SWAP = [(0, 1), (1, 0)]
LANES = 128
EXTRA = 8

VMEM = pl.BlockSpec(memory_space=pltpu.VMEM)
SMEM = pl.BlockSpec(memory_space=pltpu.SMEM)


def project(rows, basis):
    return jnp.dot(rows, basis, preferred_element_type=jnp.float32).astype(jnp.bfloat16)


def train_kernel(ids_ref, in_ref, out_ref, in_basis_ref, out_basis_ref, packed_ref):
    tokens, width = in_ref.shape
    inside = project(in_ref[...].astype(jnp.bfloat16), in_basis_ref[...])
    outside = project(out_ref[...].astype(jnp.bfloat16), out_basis_ref[...])
    for at, side in ((0, inside), (width // LANES, outside)):
        for c in range(width // LANES):
            packed_ref[(at + c) * tokens : (at + c + 1) * tokens] = side[:, c * LANES : (c + 1) * LANES]
    row = lax.broadcasted_iota(jnp.int32, (EXTRA, LANES), 0)
    lane = lax.broadcasted_iota(jnp.int32, (EXTRA, LANES), 1)
    hit = (row == 0) & (lane == ids_ref[0])
    for s in range(1, ids_ref.shape[0]):
        hit = hit | ((row == s) & (lane == ids_ref[s]))
    packed_ref[packed_ref.shape[0] - EXTRA :] = jnp.where(hit, 1.0, 0.0).astype(jnp.bfloat16)


def pack_train(train_ids, train_in, train_out, in_basis, out_basis):
    tokens, width = train_in.shape
    return pl.pallas_call(
        train_kernel,
        out_shape=jax.ShapeDtypeStruct((2 * tokens * width // LANES + EXTRA, LANES), jnp.bfloat16),
        in_specs=[SMEM] + [VMEM] * 4,
        out_specs=VMEM,
    )(train_ids, train_in, train_out, in_basis, out_basis)


def packed_scores(packed_ref, preconds, length, columns):
    end = packed_ref.shape[0] - EXTRA
    tokens = end * LANES // (2 * preconds[0].shape[0])
    seqs = tokens // length
    blocks = [packed_ref[at : at + tokens] for at in range(0, end, tokens)]
    inside = jnp.concatenate(blocks[: len(blocks) // 2], axis=1).astype(jnp.float32)
    outside = jnp.concatenate(blocks[len(blocks) // 2 :], axis=1)
    hot = packed_ref[end:].astype(jnp.float32)
    rows = [[] for _ in range(seqs)]
    for precond in preconds:
        prod = inside * jnp.dot(outside, precond[...], preferred_element_type=jnp.float32)
        for s in range(seqs):
            rows[s].append(jnp.sum(prod[s * length : (s + 1) * length], axis=0, keepdims=True))
    total = None
    for s in range(seqs):
        sums = jnp.sum(jnp.concatenate(rows[s], axis=0), axis=1, keepdims=True)
        placed = sums * hot[s : s + 1, :columns]
        total = placed if total is None else total + placed
    return total


class Arriving:
    def __init__(self, ref, copy):
        self.ref, self.copy, self.shape = ref, copy, ref.shape

    def __getitem__(self, at):
        self.copy.wait()
        return self.ref[at]


def first_scores(packed, preconds, length, columns):
    count = len(preconds)

    def kernel(packed_ref, *refs):
        stack_ref, out_ref, sems = refs[-3:]
        copies = [
            pltpu.make_async_copy(refs[q], stack_ref.at[q], sems.at[q]) for q in range(count)
        ]
        for copy in copies:
            copy.start()
        arriving = [Arriving(stack_ref.at[q], copies[q]) for q in range(count)]
        out_ref[...] = packed_scores(packed_ref, arriving, length, columns)

    return pl.pallas_call(
        kernel,
        out_shape=[
            jax.ShapeDtypeStruct((count,) + preconds[0].shape, jnp.bfloat16),
            jax.ShapeDtypeStruct((count, columns), jnp.float32),
        ],
        in_specs=[VMEM] + [pl.BlockSpec(memory_space=pl.ANY)] * count,
        out_specs=[VMEM] * 2,
        scratch_shapes=[pltpu.SemaphoreType.DMA((count,))],
        compiler_params=pltpu.CompilerParams(vmem_limit_bytes=40 << 20),
    )(packed, *preconds)


def last_scores(late, early, stack, before, length, columns):
    def kernel(late_ref, early_ref, stack_ref, before_ref, out_ref, packed_ref):
        packed_ref[...] = late_ref[...] + early_ref[...]
        preconds = [stack_ref.at[q] for q in range(stack_ref.shape[0])]
        out_ref[...] = before_ref[...] + packed_scores(packed_ref, preconds, length, columns)

    return pl.pallas_call(
        kernel,
        out_shape=jax.ShapeDtypeStruct(before.shape, jnp.float32),
        in_specs=[VMEM] * 4,
        out_specs=VMEM,
        scratch_shapes=[pltpu.VMEM(late.shape, late.dtype)],
        compiler_params=pltpu.CompilerParams(vmem_limit_bytes=40 << 20),
    )(late, early, stack, before)


def precondition(query_in, query_out, in_basis, out_basis, eigen_values):
    side_in = project(query_in, in_basis)
    side_out = project(query_out, out_basis)
    moment = lax.dot_general(
        side_out, side_in, (((0,), (0,)), ((), ())), preferred_element_type=jnp.float32
    )
    scale = query_in.shape[0] * (eigen_values + damping)
    return (moment / scale).astype(jnp.bfloat16)


def gather_preconds(precond):
    one, two, three = [
        lax.ppermute(precond, "x", [(i, i ^ step) for i in range(X)]) for step in range(1, X)
    ]
    precond, one = lax.optimization_barrier((precond, one))
    other = lax.ppermute(precond, "core", SWAP)
    one, other = lax.optimization_barrier((one, other))
    return [precond, one, two, three, other] + [
        lax.ppermute(p, "core", SWAP) for p in (one, two, three)
    ]


def swap_half(packed, places):
    pairs = [(z * ZHI + i, z * ZHI + j) for z in places for i, j in SWAP]
    return lax.ppermute(packed, ("zlo", "zhi"), pairs)


def local(
    train_in,
    train_out,
    query_in,
    query_out,
    basis_in,
    basis_out,
    eigen_values,
    train_ids,
    query_ids,
):
    in_basis = basis_in[0]
    out_basis = basis_out[0]
    seqs, length, width = train_in.shape[1:]
    columns = seqs * ZHI * X * CORE
    tokens = (seqs * length, width)

    mine = pack_train(
        train_ids, train_in[0].reshape(tokens), train_out[0].reshape(tokens), in_basis, out_basis
    )
    late = swap_half(mine, range(ZLO // 2, ZLO))
    precond = precondition(query_in[0, 0], query_out[0, 0], in_basis, out_basis, eigen_values[0])
    again, precond = lax.optimization_barrier((mine, precond))
    early = swap_half(again, range(ZLO // 2))
    preconds = lax.cond(
        lax.axis_index("x") < X, gather_preconds, lambda precond: [precond] * (X * CORE), precond
    )
    stack, partial_mine = first_scores(mine, preconds, length, columns)
    partial_value = last_scores(late, early, stack, partial_mine, length, columns)

    k = jnp.arange(X * CORE, dtype=jnp.int32)
    owner = (lax.axis_index("x") ^ (k % X)) * CORE + (lax.axis_index("core") ^ (k // X))
    order = owner[None, :] == k[:, None]
    ordered = jnp.sum(
        jnp.where(order[:, :, None], partial_value[None, :, :], 0.0), axis=1
    )
    spread = jnp.broadcast_to(ordered[None], (Y,) + ordered.shape).reshape(Y * X * CORE, -1)
    near = jnp.sum(lax.all_to_all(spread, ("y", "x", "core"), 0, 0), axis=0)
    far = jnp.broadcast_to(near[None], (ZLO,) + near.shape)
    summed = jnp.sum(lax.all_to_all(far, "zlo", 0, 0), axis=0)
    factor = 1.0 / math.sqrt(ZLO * Y * in_basis.shape[0] * out_basis.shape[0])
    scores = (summed * factor)[None, :]
    seat = jnp.arange(columns, dtype=jnp.int32)
    return jnp.where(query_ids[:, None] == seat[None, :], 0.0, scores)


def solution(mesh):
    split = Mesh(mesh.devices.reshape(ZLO, Y, ZHI, X, CORE), NAMES)
    layer, blk = ("zlo", "y"), ("zhi", "x", "core")
    placed = (
        P(layer, blk, None, None),
        P(layer, blk, None, None),
        P(layer, blk, None, None),
        P(layer, blk, None, None),
        P(layer, None, None),
        P(layer, None, None),
        P(layer, None, None),
        P(blk),
        P(blk),
    )
    return jax.shard_map(
        local, mesh=split, in_specs=placed, out_specs=P(blk, None), check_vma=False
    )
```

```python
import math

import jax
import jax.numpy as jnp
from jax import lax
from jax.experimental import pallas as pl
from jax.experimental.pallas import tpu as pltpu
from jax.sharding import Mesh
from jax.sharding import PartitionSpec as P

damping = 0.1

ZLO, Y, ZHI, X, CORE = 16, 4, 2, 4, 2
NAMES = ("zlo", "y", "zhi", "x", "core")
SWAP = [(0, 1), (1, 0)]
LANES = 128
EXTRA = 8

VMEM = pl.BlockSpec(memory_space=pltpu.VMEM)
SMEM = pl.BlockSpec(memory_space=pltpu.SMEM)


def project(rows, basis):
    return jnp.dot(rows, basis, preferred_element_type=jnp.float32).astype(jnp.bfloat16)


def train_kernel(ids_ref, in_ref, out_ref, in_basis_ref, out_basis_ref, packed_ref):
    tokens, width = in_ref.shape
    inside = project(in_ref[...].astype(jnp.bfloat16), in_basis_ref[...])
    outside = project(out_ref[...].astype(jnp.bfloat16), out_basis_ref[...])
    for at, side in ((0, inside), (width // LANES, outside)):
        for c in range(width // LANES):
            packed_ref[(at + c) * tokens : (at + c + 1) * tokens] = side[:, c * LANES : (c + 1) * LANES]
    row = lax.broadcasted_iota(jnp.int32, (EXTRA, LANES), 0)
    lane = lax.broadcasted_iota(jnp.int32, (EXTRA, LANES), 1)
    hit = (row == 0) & (lane == ids_ref[0])
    for s in range(1, ids_ref.shape[0]):
        hit = hit | ((row == s) & (lane == ids_ref[s]))
    packed_ref[packed_ref.shape[0] - EXTRA :] = jnp.where(hit, 1.0, 0.0).astype(jnp.bfloat16)


def pack_train(train_ids, train_in, train_out, in_basis, out_basis):
    tokens, width = train_in.shape
    return pl.pallas_call(
        train_kernel,
        out_shape=jax.ShapeDtypeStruct((2 * tokens * width // LANES + EXTRA, LANES), jnp.bfloat16),
        in_specs=[SMEM] + [VMEM] * 4,
        out_specs=VMEM,
        cost_estimate=pl.CostEstimate(
            flops=400 * tokens * width * width, transcendentals=0, bytes_accessed=12 * tokens * width
        ),
    )(train_ids, train_in, train_out, in_basis, out_basis)


def packed_scores(packed_ref, preconds, length, columns):
    end = packed_ref.shape[0] - EXTRA
    tokens = end * LANES // (2 * preconds[0].shape[0])
    seqs = tokens // length
    blocks = [packed_ref[at : at + tokens] for at in range(0, end, tokens)]
    inside = jnp.concatenate(blocks[: len(blocks) // 2], axis=1).astype(jnp.float32)
    outside = jnp.concatenate(blocks[len(blocks) // 2 :], axis=1)
    hot = packed_ref[end:].astype(jnp.float32)
    rows = [[] for _ in range(seqs)]
    for precond in preconds:
        prod = inside * jnp.dot(outside, precond[...], preferred_element_type=jnp.float32)
        for s in range(seqs):
            rows[s].append(jnp.sum(prod[s * length : (s + 1) * length], axis=0, keepdims=True))
    total = None
    for s in range(seqs):
        sums = jnp.sum(jnp.concatenate(rows[s], axis=0), axis=1, keepdims=True)
        placed = sums * hot[s : s + 1, :columns]
        total = placed if total is None else total + placed
    return total


class Arriving:
    def __init__(self, ref, copy):
        self.ref, self.copy, self.shape = ref, copy, ref.shape

    def __getitem__(self, at):
        self.copy.wait()
        return self.ref[at]


def first_scores(packed, preconds, length, columns):
    count = len(preconds)

    def kernel(packed_ref, *refs):
        stack_ref, out_ref, sems = refs[-3:]
        copies = [
            pltpu.make_async_copy(refs[q], stack_ref.at[q], sems.at[q]) for q in range(count)
        ]
        for copy in copies:
            copy.start()
        arriving = [Arriving(stack_ref.at[q], copies[q]) for q in range(count)]
        out_ref[...] = packed_scores(packed_ref, arriving, length, columns)

    return pl.pallas_call(
        kernel,
        out_shape=[
            jax.ShapeDtypeStruct((count,) + preconds[0].shape, jnp.bfloat16),
            jax.ShapeDtypeStruct((count, columns), jnp.float32),
        ],
        in_specs=[VMEM] + [pl.BlockSpec(memory_space=pl.ANY)] * count,
        out_specs=[VMEM] * 2,
        scratch_shapes=[pltpu.SemaphoreType.DMA((count,))],
        compiler_params=pltpu.CompilerParams(vmem_limit_bytes=40 << 20),
    )(packed, *preconds)


def last_scores(late, early, token, stack, before, length, columns):
    def kernel(late_ref, early_ref, token_ref, stack_ref, before_ref, out_ref, packed_ref):
        packed_ref[...] = late_ref[...] + early_ref[...]
        preconds = [stack_ref.at[q] for q in range(stack_ref.shape[0])]
        out_ref[...] = before_ref[...] + packed_scores(packed_ref, preconds, length, columns)

    return pl.pallas_call(
        kernel,
        out_shape=jax.ShapeDtypeStruct(before.shape, jnp.float32),
        in_specs=[VMEM] * 5,
        out_specs=VMEM,
        scratch_shapes=[pltpu.VMEM(late.shape, late.dtype)],
        compiler_params=pltpu.CompilerParams(vmem_limit_bytes=40 << 20),
    )(late, early, token, stack, before)


def precondition(query_in, query_out, in_basis, out_basis, eigen_values):
    side_in = project(query_in, in_basis)
    side_out = project(query_out, out_basis)
    moment = lax.dot_general(
        side_out, side_in, (((0,), (0,)), ((), ())), preferred_element_type=jnp.float32
    )
    scale = query_in.shape[0] * (eigen_values + damping)
    return (moment / scale).astype(jnp.bfloat16)


def gather_preconds(precond):
    one, two, three = [
        lax.ppermute(precond, "x", [(i, i ^ step) for i in range(X)]) for step in range(1, X)
    ]
    precond, one = lax.optimization_barrier((precond, one))
    other = lax.ppermute(precond, "core", SWAP)
    one, other = lax.optimization_barrier((one, other))
    return [precond, one, two, three, other] + [
        lax.ppermute(p, "core", SWAP) for p in (one, two, three)
    ]


def swap_half(packed, places):
    pairs = [(z * ZHI + i, z * ZHI + j) for z in places for i, j in SWAP]
    return lax.ppermute(packed, ("zlo", "zhi"), pairs)


def local(
    train_in,
    train_out,
    query_in,
    query_out,
    basis_in,
    basis_out,
    eigen_values,
    train_ids,
    query_ids,
):
    in_basis = basis_in[0]
    out_basis = basis_out[0]
    seqs, length, width = train_in.shape[1:]
    columns = seqs * ZHI * X * CORE
    tokens = (seqs * length, width)

    mine = pack_train(
        train_ids, train_in[0].reshape(tokens), train_out[0].reshape(tokens), in_basis, out_basis
    )
    late = swap_half(mine, range(ZLO // 2, ZLO))
    precond = precondition(query_in[0, 0], query_out[0, 0], in_basis, out_basis, eigen_values[0])
    token = lax.ppermute(
        mine[:EXTRA],
        ("zlo", "core"),
        [(z * CORE + i, z * CORE + j) for z in range(ZLO // 2) for i, j in SWAP],
    )
    again, precond, token = lax.optimization_barrier((mine, precond, token))
    early = swap_half(again, range(ZLO // 2))
    preconds = lax.cond(
        lax.axis_index("x") < X, gather_preconds, lambda precond: [precond] * (X * CORE), precond
    )
    stack, partial_mine = first_scores(mine, preconds, length, columns)
    partial_value = last_scores(late, early, token, stack, partial_mine, length, columns)

    k = jnp.arange(X * CORE, dtype=jnp.int32)
    owner = (lax.axis_index("x") ^ (k % X)) * CORE + (lax.axis_index("core") ^ (k // X))
    order = owner[None, :] == k[:, None]
    ordered = jnp.sum(
        jnp.where(order[:, :, None], partial_value[None, :, :], 0.0), axis=1
    )
    spread = jnp.broadcast_to(ordered[None], (Y,) + ordered.shape).reshape(Y * X * CORE, -1)
    near = jnp.sum(lax.all_to_all(spread, ("y", "x", "core"), 0, 0), axis=0)
    far = jnp.broadcast_to(near[None], (ZLO,) + near.shape)
    summed = jnp.sum(lax.all_to_all(far, "zlo", 0, 0), axis=0)
    factor = 1.0 / math.sqrt(ZLO * Y * in_basis.shape[0] * out_basis.shape[0])
    scores = (summed * factor)[None, :]
    seat = jnp.arange(columns, dtype=jnp.int32)
    return jnp.where(query_ids[:, None] == seat[None, :], 0.0, scores)


def solution(mesh):
    split = Mesh(mesh.devices.reshape(ZLO, Y, ZHI, X, CORE), NAMES)
    layer, blk = ("zlo", "y"), ("zhi", "x", "core")
    placed = (
        P(layer, blk, None, None),
        P(layer, blk, None, None),
        P(layer, blk, None, None),
        P(layer, blk, None, None),
        P(layer, None, None),
        P(layer, None, None),
        P(layer, None, None),
        P(blk),
        P(blk),
    )
    return jax.shard_map(
        local, mesh=split, in_specs=placed, out_specs=P(blk, None), check_vma=False
    )
```

```python
import math

import jax
import jax.numpy as jnp
from jax import lax
from jax.experimental import pallas as pl
from jax.experimental.pallas import tpu as pltpu
from jax.sharding import Mesh
from jax.sharding import PartitionSpec as P

damping = 0.1

ZLO, Y, ZHI, X, CORE = 16, 4, 2, 4, 2
NAMES = ("zlo", "y", "zhi", "x", "core")
SWAP = [(0, 1), (1, 0)]
LANES = 128
EXTRA = 8

VMEM = pl.BlockSpec(memory_space=pltpu.VMEM)
SMEM = pl.BlockSpec(memory_space=pltpu.SMEM)


def project(rows, basis):
    return jnp.dot(rows, basis, preferred_element_type=jnp.float32).astype(jnp.bfloat16)


def train_kernel(ids_ref, in_ref, out_ref, in_basis_ref, out_basis_ref, packed_ref):
    tokens, width = in_ref.shape
    inside = project(in_ref[...].astype(jnp.bfloat16), in_basis_ref[...])
    outside = project(out_ref[...].astype(jnp.bfloat16), out_basis_ref[...])
    for at, side in ((0, inside), (width // LANES, outside)):
        for c in range(width // LANES):
            packed_ref[(at + c) * tokens : (at + c + 1) * tokens] = side[:, c * LANES : (c + 1) * LANES]
    row = lax.broadcasted_iota(jnp.int32, (EXTRA, LANES), 0)
    lane = lax.broadcasted_iota(jnp.int32, (EXTRA, LANES), 1)
    hit = (row == 0) & (lane == ids_ref[0])
    for s in range(1, ids_ref.shape[0]):
        hit = hit | ((row == s) & (lane == ids_ref[s]))
    packed_ref[packed_ref.shape[0] - EXTRA :] = jnp.where(hit, 1.0, 0.0).astype(jnp.bfloat16)


def pack_train(train_ids, train_in, train_out, in_basis, out_basis):
    tokens, width = train_in.shape
    return pl.pallas_call(
        train_kernel,
        out_shape=jax.ShapeDtypeStruct((2 * tokens * width // LANES + EXTRA, LANES), jnp.bfloat16),
        in_specs=[SMEM] + [VMEM] * 4,
        out_specs=VMEM,
        cost_estimate=pl.CostEstimate(
            flops=400 * tokens * width * width, transcendentals=0, bytes_accessed=12 * tokens * width
        ),
    )(train_ids, train_in, train_out, in_basis, out_basis)


def packed_scores(packed_ref, preconds, length, columns):
    end = packed_ref.shape[0] - EXTRA
    tokens = end * LANES // (2 * preconds[0].shape[0])
    seqs = tokens // length
    blocks = [packed_ref[at : at + tokens] for at in range(0, end, tokens)]
    inside = jnp.concatenate(blocks[: len(blocks) // 2], axis=1).astype(jnp.float32)
    outside = jnp.concatenate(blocks[len(blocks) // 2 :], axis=1)
    hot = packed_ref[end:].astype(jnp.float32)
    rows = [[] for _ in range(seqs)]
    for precond in preconds:
        prod = inside * jnp.dot(outside, precond[...], preferred_element_type=jnp.float32)
        for s in range(seqs):
            rows[s].append(jnp.sum(prod[s * length : (s + 1) * length], axis=0, keepdims=True))
    total = None
    for s in range(seqs):
        sums = jnp.sum(jnp.concatenate(rows[s], axis=0), axis=1, keepdims=True)
        placed = sums * hot[s : s + 1, :columns]
        total = placed if total is None else total + placed
    return total


class Arriving:
    def __init__(self, ref, copy):
        self.ref, self.copy, self.shape = ref, copy, ref.shape

    def __getitem__(self, at):
        self.copy.wait()
        return self.ref[at]


def first_scores(packed, preconds, length, columns):
    count = len(preconds)

    def kernel(packed_ref, *refs):
        stack_ref, out_ref, sems = refs[-3:]
        copies = [
            pltpu.make_async_copy(refs[q], stack_ref.at[q], sems.at[q]) for q in range(count)
        ]
        for copy in copies:
            copy.start()
        arriving = [Arriving(stack_ref.at[q], copies[q]) for q in range(count)]
        out_ref[...] = packed_scores(packed_ref, arriving, length, columns)

    return pl.pallas_call(
        kernel,
        out_shape=[
            jax.ShapeDtypeStruct((count,) + preconds[0].shape, jnp.bfloat16),
            jax.ShapeDtypeStruct((count, columns), jnp.float32),
        ],
        in_specs=[VMEM] + [pl.BlockSpec(memory_space=pl.ANY)] * count,
        out_specs=[VMEM] * 2,
        scratch_shapes=[pltpu.SemaphoreType.DMA((count,))],
        compiler_params=pltpu.CompilerParams(vmem_limit_bytes=40 << 20),
    )(packed, *preconds)


def last_scores(late, early, token, stack, before, length, columns):
    def kernel(late_ref, early_ref, token_ref, stack_ref, before_ref, out_ref, packed_ref):
        packed_ref[...] = late_ref[...] + early_ref[...]
        preconds = [stack_ref.at[q] for q in range(stack_ref.shape[0])]
        out_ref[...] = before_ref[...] + packed_scores(packed_ref, preconds, length, columns)

    return pl.pallas_call(
        kernel,
        out_shape=jax.ShapeDtypeStruct(before.shape, jnp.float32),
        in_specs=[VMEM] * 5,
        out_specs=VMEM,
        scratch_shapes=[pltpu.VMEM(late.shape, late.dtype)],
        compiler_params=pltpu.CompilerParams(vmem_limit_bytes=40 << 20),
    )(late, early, token, stack, before)


def precondition(query_in, query_out, in_basis, out_basis, eigen_values):
    side_in = project(query_in, in_basis)
    side_out = project(query_out, out_basis)
    moment = lax.dot_general(
        side_out, side_in, (((0,), (0,)), ((), ())), preferred_element_type=jnp.float32
    )
    scale = query_in.shape[0] * (eigen_values + damping)
    return (moment / scale).astype(jnp.bfloat16)


def gather_preconds(precond):
    other = lax.ppermute(precond, "core", SWAP)
    again, other = lax.optimization_barrier((precond, other))
    along = [
        lax.ppermute(again if step == 1 else precond, "x", [(i, i ^ step) for i in range(X)])
        for step in range(1, X)
    ]
    beside = [lax.ppermute(p, "core", SWAP) for p in along]
    return [precond] + along + [other] + beside


def swap_half(packed, places):
    pairs = [(z * ZHI + i, z * ZHI + j) for z in places for i, j in SWAP]
    return lax.ppermute(packed, ("zlo", "zhi"), pairs)


def local(
    train_in,
    train_out,
    query_in,
    query_out,
    basis_in,
    basis_out,
    eigen_values,
    train_ids,
    query_ids,
):
    in_basis = basis_in[0]
    out_basis = basis_out[0]
    seqs, length, width = train_in.shape[1:]
    columns = seqs * ZHI * X * CORE
    tokens = (seqs * length, width)

    mine = pack_train(
        train_ids, train_in[0].reshape(tokens), train_out[0].reshape(tokens), in_basis, out_basis
    )
    late = swap_half(mine, range(ZLO // 2, ZLO))
    precond = precondition(query_in[0, 0], query_out[0, 0], in_basis, out_basis, eigen_values[0])
    token = lax.ppermute(
        mine[:EXTRA],
        ("zlo", "core"),
        [(z * CORE + i, z * CORE + j) for z in range(ZLO // 2) for i, j in SWAP],
    )
    again, precond, token = lax.optimization_barrier((mine, precond, token))
    early = swap_half(again, range(ZLO // 2))
    preconds = lax.cond(
        lax.axis_index("x") < X, gather_preconds, lambda precond: [precond] * (X * CORE), precond
    )
    stack, partial_mine = first_scores(mine, preconds, length, columns)
    partial_value = last_scores(late, early, token, stack, partial_mine, length, columns)

    k = jnp.arange(X * CORE, dtype=jnp.int32)
    owner = (lax.axis_index("x") ^ (k % X)) * CORE + (lax.axis_index("core") ^ (k // X))
    order = owner[None, :] == k[:, None]
    ordered = jnp.sum(
        jnp.where(order[:, :, None], partial_value[None, :, :], 0.0), axis=1
    )
    spread = jnp.broadcast_to(ordered[None], (Y,) + ordered.shape).reshape(Y * X * CORE, -1)
    near = jnp.sum(lax.all_to_all(spread, ("y", "x", "core"), 0, 0), axis=0)
    far = jnp.broadcast_to(near[None], (ZLO,) + near.shape)
    summed = jnp.sum(lax.all_to_all(far, "zlo", 0, 0), axis=0)
    factor = 1.0 / math.sqrt(ZLO * Y * in_basis.shape[0] * out_basis.shape[0])
    scores = (summed * factor)[None, :]
    seat = jnp.arange(columns, dtype=jnp.int32)
    return jnp.where(query_ids[:, None] == seat[None, :], 0.0, scores)


def solution(mesh):
    split = Mesh(mesh.devices.reshape(ZLO, Y, ZHI, X, CORE), NAMES)
    layer, blk = ("zlo", "y"), ("zhi", "x", "core")
    placed = (
        P(layer, blk, None, None),
        P(layer, blk, None, None),
        P(layer, blk, None, None),
        P(layer, blk, None, None),
        P(layer, None, None),
        P(layer, None, None),
        P(layer, None, None),
        P(blk),
        P(blk),
    )
    return jax.shard_map(
        local, mesh=split, in_specs=placed, out_specs=P(blk, None), check_vma=False
    )
```

```python
import math

import jax
import jax.numpy as jnp
from jax import lax
from jax.experimental import pallas as pl
from jax.experimental.pallas import tpu as pltpu
from jax.sharding import Mesh
from jax.sharding import PartitionSpec as P

damping = 0.1

ZLO, Y, ZHI, X, CORE = 16, 4, 2, 4, 2
NAMES = ("zlo", "y", "zhi", "x", "core")
SWAP = [(0, 1), (1, 0)]
LANES = 128
EXTRA = 8

VMEM = pl.BlockSpec(memory_space=pltpu.VMEM)
SMEM = pl.BlockSpec(memory_space=pltpu.SMEM)


def project(rows, basis):
    return jnp.dot(rows, basis, preferred_element_type=jnp.float32).astype(jnp.bfloat16)


def train_kernel(ids_ref, in_ref, out_ref, in_basis_ref, out_basis_ref, packed_ref):
    tokens, width = in_ref.shape
    inside = project(in_ref[...].astype(jnp.bfloat16), in_basis_ref[...])
    outside = project(out_ref[...].astype(jnp.bfloat16), out_basis_ref[...])
    for at, side in ((0, inside), (width // LANES, outside)):
        for c in range(width // LANES):
            packed_ref[(at + c) * tokens : (at + c + 1) * tokens] = side[:, c * LANES : (c + 1) * LANES]
    row = lax.broadcasted_iota(jnp.int32, (EXTRA, LANES), 0)
    lane = lax.broadcasted_iota(jnp.int32, (EXTRA, LANES), 1)
    hit = (row == 0) & (lane == ids_ref[0])
    for s in range(1, ids_ref.shape[0]):
        hit = hit | ((row == s) & (lane == ids_ref[s]))
    packed_ref[packed_ref.shape[0] - EXTRA :] = jnp.where(hit, 1.0, 0.0).astype(jnp.bfloat16)


def pack_train(train_ids, train_in, train_out, in_basis, out_basis):
    tokens, width = train_in.shape
    return pl.pallas_call(
        train_kernel,
        out_shape=jax.ShapeDtypeStruct((2 * tokens * width // LANES + EXTRA, LANES), jnp.bfloat16),
        in_specs=[SMEM] + [VMEM] * 4,
        out_specs=VMEM,
        cost_estimate=pl.CostEstimate(
            flops=400 * tokens * width * width, transcendentals=0, bytes_accessed=12 * tokens * width
        ),
    )(train_ids, train_in, train_out, in_basis, out_basis)


def packed_scores(packed_ref, preconds, length, columns):
    end = packed_ref.shape[0] - EXTRA
    tokens = end * LANES // (2 * preconds[0].shape[0])
    seqs = tokens // length
    blocks = [packed_ref[at : at + tokens] for at in range(0, end, tokens)]
    inside = jnp.concatenate(blocks[: len(blocks) // 2], axis=1).astype(jnp.float32)
    outside = jnp.concatenate(blocks[len(blocks) // 2 :], axis=1)
    hot = packed_ref[end:].astype(jnp.float32)
    rows = [[] for _ in range(seqs)]
    for precond in preconds:
        prod = inside * jnp.dot(outside, precond[...], preferred_element_type=jnp.float32)
        for s in range(seqs):
            rows[s].append(jnp.sum(prod[s * length : (s + 1) * length], axis=0, keepdims=True))
    total = None
    for s in range(seqs):
        sums = jnp.sum(jnp.concatenate(rows[s], axis=0), axis=1, keepdims=True)
        placed = sums * hot[s : s + 1, :columns]
        total = placed if total is None else total + placed
    return total


class Arriving:
    def __init__(self, ref, copy):
        self.ref, self.copy, self.shape = ref, copy, ref.shape

    def __getitem__(self, at):
        self.copy.wait()
        return self.ref[at]


def first_scores(packed, preconds, length, columns):
    count = len(preconds)

    def kernel(packed_ref, *refs):
        stack_ref, out_ref, sems = refs[-3:]
        copies = [
            pltpu.make_async_copy(refs[q], stack_ref.at[q], sems.at[q]) for q in range(count)
        ]
        for copy in copies:
            copy.start()
        arriving = [Arriving(stack_ref.at[q], copies[q]) for q in range(count)]
        out_ref[...] = packed_scores(packed_ref, arriving, length, columns)

    return pl.pallas_call(
        kernel,
        out_shape=[
            jax.ShapeDtypeStruct((count,) + preconds[0].shape, jnp.bfloat16),
            jax.ShapeDtypeStruct((count, columns), jnp.float32),
        ],
        in_specs=[VMEM] + [pl.BlockSpec(memory_space=pl.ANY)] * count,
        out_specs=[VMEM] * 2,
        scratch_shapes=[pltpu.SemaphoreType.DMA((count,))],
        compiler_params=pltpu.CompilerParams(vmem_limit_bytes=40 << 20),
    )(packed, *preconds)


def last_scores(late, early, token, stack, before, length, columns):
    def kernel(late_ref, early_ref, token_ref, stack_ref, before_ref, out_ref, packed_ref):
        packed_ref[...] = late_ref[...] + early_ref[...]
        preconds = [stack_ref.at[q] for q in range(stack_ref.shape[0])]
        out_ref[...] = before_ref[...] + packed_scores(packed_ref, preconds, length, columns)

    return pl.pallas_call(
        kernel,
        out_shape=jax.ShapeDtypeStruct(before.shape, jnp.float32),
        in_specs=[VMEM] * 5,
        out_specs=VMEM,
        scratch_shapes=[pltpu.VMEM(late.shape, late.dtype)],
        compiler_params=pltpu.CompilerParams(vmem_limit_bytes=40 << 20),
    )(late, early, token, stack, before)


def precondition(query_in, query_out, in_basis, out_basis, eigen_values):
    side_in = project(query_in, in_basis)
    side_out = project(query_out, out_basis)
    moment = lax.dot_general(
        side_out, side_in, (((0,), (0,)), ((), ())), preferred_element_type=jnp.float32
    )
    scale = query_in.shape[0] * (eigen_values + damping)
    return (moment / scale).astype(jnp.bfloat16)


def gather_preconds(precond):
    other = lax.ppermute(precond, "core", SWAP)
    again, other = lax.optimization_barrier((precond, other))
    along = [
        lax.ppermute(again if step == 1 else precond, "x", [(i, i ^ step) for i in range(X)])
        for step in range(1, X)
    ]
    beside = [lax.ppermute(p, "core", SWAP) for p in along]
    return [precond] + along + [other] + beside


def swap_half(packed, places):
    pairs = [(z * ZHI + i, z * ZHI + j) for z in places for i, j in SWAP]
    return lax.ppermute(packed, ("zlo", "zhi"), pairs)


def local(
    train_in,
    train_out,
    query_in,
    query_out,
    basis_in,
    basis_out,
    eigen_values,
    train_ids,
    query_ids,
):
    in_basis = basis_in[0]
    out_basis = basis_out[0]
    seqs, length, width = train_in.shape[1:]
    columns = seqs * ZHI * X * CORE
    tokens = (seqs * length, width)

    mine = pack_train(
        train_ids, train_in[0].reshape(tokens), train_out[0].reshape(tokens), in_basis, out_basis
    )
    late = swap_half(mine, range(ZLO // 2, ZLO))
    precond = precondition(query_in[0, 0], query_out[0, 0], in_basis, out_basis, eigen_values[0])
    token = mine[:EXTRA]
    for _ in range(2):
        token = lax.ppermute(
            token,
            ("zlo", "core"),
            [(z * CORE + i, z * CORE + j) for z in range(ZLO // 2) for i, j in SWAP],
        )
    again, precond, token = lax.optimization_barrier((mine, precond, token))
    early = swap_half(again, range(ZLO // 2))
    preconds = lax.cond(
        lax.axis_index("x") < X, gather_preconds, lambda precond: [precond] * (X * CORE), precond
    )
    stack, partial_mine = first_scores(mine, preconds, length, columns)
    partial_value = last_scores(late, early, token, stack, partial_mine, length, columns)

    k = jnp.arange(X * CORE, dtype=jnp.int32)
    owner = (lax.axis_index("x") ^ (k % X)) * CORE + (lax.axis_index("core") ^ (k // X))
    order = owner[None, :] == k[:, None]
    ordered = jnp.sum(
        jnp.where(order[:, :, None], partial_value[None, :, :], 0.0), axis=1
    )
    spread = jnp.broadcast_to(ordered[None], (Y,) + ordered.shape).reshape(Y * X * CORE, -1)
    near = jnp.sum(lax.all_to_all(spread, ("y", "x", "core"), 0, 0), axis=0)
    far = jnp.broadcast_to(near[None], (ZLO,) + near.shape)
    summed = jnp.sum(lax.all_to_all(far, "zlo", 0, 0), axis=0)
    factor = 1.0 / math.sqrt(ZLO * Y * in_basis.shape[0] * out_basis.shape[0])
    scores = (summed * factor)[None, :]
    seat = jnp.arange(columns, dtype=jnp.int32)
    return jnp.where(query_ids[:, None] == seat[None, :], 0.0, scores)


def solution(mesh):
    split = Mesh(mesh.devices.reshape(ZLO, Y, ZHI, X, CORE), NAMES)
    layer, blk = ("zlo", "y"), ("zhi", "x", "core")
    placed = (
        P(layer, blk, None, None),
        P(layer, blk, None, None),
        P(layer, blk, None, None),
        P(layer, blk, None, None),
        P(layer, None, None),
        P(layer, None, None),
        P(layer, None, None),
        P(blk),
        P(blk),
    )
    return jax.shard_map(
        local, mesh=split, in_specs=placed, out_specs=P(blk, None), check_vma=False
    )
```

```python
import math

import jax
import jax.numpy as jnp
from jax import lax
from jax.experimental import pallas as pl
from jax.experimental.pallas import tpu as pltpu
from jax.sharding import Mesh
from jax.sharding import PartitionSpec as P

damping = 0.1

ZLO, Y, ZHI, X, CORE = 16, 4, 2, 4, 2
NAMES = ("zlo", "y", "zhi", "x", "core")
SWAP = [(0, 1), (1, 0)]
EARLY = 6
LANES = 128
EXTRA = 8

VMEM = pl.BlockSpec(memory_space=pltpu.VMEM)
SMEM = pl.BlockSpec(memory_space=pltpu.SMEM)


def project(rows, basis):
    return jnp.dot(rows, basis, preferred_element_type=jnp.float32).astype(jnp.bfloat16)


def train_kernel(ids_ref, in_ref, out_ref, in_basis_ref, out_basis_ref, packed_ref):
    tokens, width = in_ref.shape
    inside = project(in_ref[...].astype(jnp.bfloat16), in_basis_ref[...])
    outside = project(out_ref[...].astype(jnp.bfloat16), out_basis_ref[...])
    for at, side in ((0, inside), (width // LANES, outside)):
        for c in range(width // LANES):
            packed_ref[(at + c) * tokens : (at + c + 1) * tokens] = side[:, c * LANES : (c + 1) * LANES]
    row = lax.broadcasted_iota(jnp.int32, (EXTRA, LANES), 0)
    lane = lax.broadcasted_iota(jnp.int32, (EXTRA, LANES), 1)
    hit = (row == 0) & (lane == ids_ref[0])
    for s in range(1, ids_ref.shape[0]):
        hit = hit | ((row == s) & (lane == ids_ref[s]))
    packed_ref[packed_ref.shape[0] - EXTRA :] = jnp.where(hit, 1.0, 0.0).astype(jnp.bfloat16)


def pack_train(train_ids, train_in, train_out, in_basis, out_basis):
    tokens, width = train_in.shape
    return pl.pallas_call(
        train_kernel,
        out_shape=jax.ShapeDtypeStruct((2 * tokens * width // LANES + EXTRA, LANES), jnp.bfloat16),
        in_specs=[SMEM] + [VMEM] * 4,
        out_specs=VMEM,
        cost_estimate=pl.CostEstimate(
            flops=400 * tokens * width * width, transcendentals=0, bytes_accessed=12 * tokens * width
        ),
    )(train_ids, train_in, train_out, in_basis, out_basis)


def packed_scores(packed_ref, preconds, length, columns):
    end = packed_ref.shape[0] - EXTRA
    tokens = end * LANES // (2 * preconds[0].shape[0])
    seqs = tokens // length
    blocks = [packed_ref[at : at + tokens] for at in range(0, end, tokens)]
    inside = jnp.concatenate(blocks[: len(blocks) // 2], axis=1).astype(jnp.float32)
    outside = jnp.concatenate(blocks[len(blocks) // 2 :], axis=1)
    hot = packed_ref[end:].astype(jnp.float32)
    rows = [[] for _ in range(seqs)]
    for precond in preconds:
        prod = inside * jnp.dot(outside, precond[...], preferred_element_type=jnp.float32)
        for s in range(seqs):
            rows[s].append(jnp.sum(prod[s * length : (s + 1) * length], axis=0, keepdims=True))
    total = None
    for s in range(seqs):
        sums = jnp.sum(jnp.concatenate(rows[s], axis=0), axis=1, keepdims=True)
        placed = sums * hot[s : s + 1, :columns]
        total = placed if total is None else total + placed
    return total


class Arriving:
    def __init__(self, ref, copy):
        self.ref, self.copy, self.shape = ref, copy, ref.shape

    def __getitem__(self, at):
        self.copy.wait()
        return self.ref[at]


def first_scores(packed, preconds, length, columns):
    count = len(preconds)

    def kernel(packed_ref, *refs):
        stack_ref, out_ref, sems = refs[-3:]
        copies = [
            pltpu.make_async_copy(refs[q], stack_ref.at[q], sems.at[q]) for q in range(count)
        ]
        for copy in copies:
            copy.start()
        arriving = [Arriving(stack_ref.at[q], copies[q]) for q in range(count)]
        out_ref[...] = packed_scores(packed_ref, arriving, length, columns)

    return pl.pallas_call(
        kernel,
        out_shape=[
            jax.ShapeDtypeStruct((count,) + preconds[0].shape, jnp.bfloat16),
            jax.ShapeDtypeStruct((count, columns), jnp.float32),
        ],
        in_specs=[VMEM] + [pl.BlockSpec(memory_space=pl.ANY)] * count,
        out_specs=[VMEM] * 2,
        scratch_shapes=[pltpu.SemaphoreType.DMA((count,))],
        compiler_params=pltpu.CompilerParams(vmem_limit_bytes=40 << 20),
    )(packed, *preconds)


def last_scores(late, early, token, stack, before, length, columns):
    def kernel(late_ref, early_ref, token_ref, stack_ref, before_ref, out_ref, packed_ref):
        packed_ref[...] = late_ref[...] + early_ref[...]
        preconds = [stack_ref.at[q] for q in range(stack_ref.shape[0])]
        out_ref[...] = before_ref[...] + packed_scores(packed_ref, preconds, length, columns)

    return pl.pallas_call(
        kernel,
        out_shape=jax.ShapeDtypeStruct(before.shape, jnp.float32),
        in_specs=[VMEM] * 5,
        out_specs=VMEM,
        scratch_shapes=[pltpu.VMEM(late.shape, late.dtype)],
        compiler_params=pltpu.CompilerParams(vmem_limit_bytes=40 << 20),
    )(late, early, token, stack, before)


def precondition(query_in, query_out, in_basis, out_basis, eigen_values):
    side_in = project(query_in, in_basis)
    side_out = project(query_out, out_basis)
    moment = lax.dot_general(
        side_out, side_in, (((0,), (0,)), ((), ())), preferred_element_type=jnp.float32
    )
    scale = query_in.shape[0] * (eigen_values + damping)
    return (moment / scale).astype(jnp.bfloat16)


def gather_preconds(precond):
    other = lax.ppermute(precond, "core", SWAP)
    again, other = lax.optimization_barrier((precond, other))
    along = [
        lax.ppermute(again if step == 1 else precond, "x", [(i, i ^ step) for i in range(X)])
        for step in range(1, X)
    ]
    beside = [lax.ppermute(p, "core", SWAP) for p in along]
    return [precond] + along + [other] + beside


def swap_half(packed, places):
    pairs = [(z * ZHI + i, z * ZHI + j) for z in places for i, j in SWAP]
    return lax.ppermute(packed, ("zlo", "zhi"), pairs)


def local(
    train_in,
    train_out,
    query_in,
    query_out,
    basis_in,
    basis_out,
    eigen_values,
    train_ids,
    query_ids,
):
    in_basis = basis_in[0]
    out_basis = basis_out[0]
    seqs, length, width = train_in.shape[1:]
    columns = seqs * ZHI * X * CORE
    tokens = (seqs * length, width)

    mine = pack_train(
        train_ids, train_in[0].reshape(tokens), train_out[0].reshape(tokens), in_basis, out_basis
    )
    late = swap_half(mine, range(EARLY, ZLO))
    precond = precondition(query_in[0, 0], query_out[0, 0], in_basis, out_basis, eigen_values[0])
    token = lax.ppermute(
        mine[:EXTRA],
        ("zlo", "core"),
        [(z * CORE + i, z * CORE + j) for z in range(EARLY) for i, j in SWAP],
    )
    again, precond, token = lax.optimization_barrier((mine, precond, token))
    early = swap_half(again, range(EARLY))
    preconds = lax.cond(
        lax.axis_index("x") < X, gather_preconds, lambda precond: [precond] * (X * CORE), precond
    )
    stack, partial_mine = first_scores(mine, preconds, length, columns)
    partial_value = last_scores(late, early, token, stack, partial_mine, length, columns)

    k = jnp.arange(X * CORE, dtype=jnp.int32)
    owner = (lax.axis_index("x") ^ (k % X)) * CORE + (lax.axis_index("core") ^ (k // X))
    order = owner[None, :] == k[:, None]
    ordered = jnp.sum(
        jnp.where(order[:, :, None], partial_value[None, :, :], 0.0), axis=1
    )
    spread = jnp.broadcast_to(ordered[None], (Y,) + ordered.shape).reshape(Y * X * CORE, -1)
    near = jnp.sum(lax.all_to_all(spread, ("y", "x", "core"), 0, 0), axis=0)
    far = jnp.broadcast_to(near[None], (ZLO,) + near.shape)
    summed = jnp.sum(lax.all_to_all(far, "zlo", 0, 0), axis=0)
    factor = 1.0 / math.sqrt(ZLO * Y * in_basis.shape[0] * out_basis.shape[0])
    scores = (summed * factor)[None, :]
    seat = jnp.arange(columns, dtype=jnp.int32)
    return jnp.where(query_ids[:, None] == seat[None, :], 0.0, scores)


def solution(mesh):
    split = Mesh(mesh.devices.reshape(ZLO, Y, ZHI, X, CORE), NAMES)
    layer, blk = ("zlo", "y"), ("zhi", "x", "core")
    placed = (
        P(layer, blk, None, None),
        P(layer, blk, None, None),
        P(layer, blk, None, None),
        P(layer, blk, None, None),
        P(layer, None, None),
        P(layer, None, None),
        P(layer, None, None),
        P(blk),
        P(blk),
    )
    return jax.shard_map(
        local, mesh=split, in_specs=placed, out_specs=P(blk, None), check_vma=False
    )
```
